256 devices in a mesh: arm: 4 (over x_hi, core), space: 64 (over y, x_lo, z).
Axes of the slice: x: 4 (x_hi: 2, x_lo: 2; x = x_hi * 2 + x_lo), y: 4, z: 8, core: 2. Of those that a mesh axis runs over, the one named last changes fastest.
Arguments:
- fields: float32 [2, 256, 64, 128], P(None, 'space'), may hold values from -2.5 to 2.5
- starts: float32 [16, 256, 64, 128], P('arm', 'space'), may hold values from 0.6 to 1.4
- labels: int32 [16], P('arm'), may hold values from 0 to 1
Outputs:
- density: float32 [2, 256, 64, 128], P(None, 'space', 'arm')
- new_fields: float32 [2, 256, 64, 128], P(None, 'space', 'arm')
The draws below stay inside these ranges and needn't reach their ends.
All inputs are finite; a program needn't handle non-finite values.
Results may differ from the reference program's by a relative error of at most 0.0003.
Values sent between devices are 32-bit elements; how exact they have to be, the bound alone decides.
A program may use at most 64 MiB of HBM per device.

```python
import jax
import jax.numpy as jnp
from jax import lax

NY = 64
NZ = 128
ARMS = 16
NX = 256


def draw_fields(key, part):
    key_rough, key_level = jax.random.split(key, 2)
    levels = jax.random.uniform(key_level, (2, NX, 1, 1), jnp.float32, -1.2, 1.2)
    roughness = 0.55 * jnp.clip(jax.random.normal(key_rough, (2, NX, NY, NZ), jnp.float32), -2.0, 2.0)
    return levels + roughness


def set_ends(result, own_key, smallest, largest):
    shape = result.shape
    spot = [jax.random.randint(jax.random.fold_in(own_key, axis), (), 0, shape[axis]) for axis in range(len(shape))]
    result = result.at[tuple(spot)].set(smallest)
    longest = shape.index(max(shape))
    spot[longest] = (spot[longest] + 1) % shape[longest]
    return result.at[tuple(spot)].set(largest)


def level_of(rng, shape, cuts, least, largest):
    def one(axis_at, shards_of):
        steps = jax.random.uniform(jax.random.fold_in(jax.random.fold_in(rng, 6), axis_at), (shards_of,), jnp.float32, least / len(cuts), largest / len(cuts))
        return jnp.repeat(jnp.exp(steps), shape[axis_at] // shards_of).reshape((-1,) + (1,) * (len(shape) - axis_at - 1))

    factor_of = one(*cuts[0])
    for cut in cuts[1:]:
        factor_of = factor_of * one(*cut)
    return factor_of


def setup_inputs(seed: int = 0) -> dict:
    streams_of = jax.random.split(jax.random.key(seed), 4)
    return {
        "fields": draw_fields(jax.random.fold_in(streams_of[3], 71), 0),
        "starts": jnp.clip(0.6 + 0.79999995 * jax.random.uniform(streams_of[1], (ARMS, NX, NY, NZ), jnp.float32) ** level_of(streams_of[1], (ARMS, NX, NY, NZ), ((0, 4), (1, 64)), -0.2, 0.2), 0.6, 1.4),
        "labels": set_ends(jax.random.randint(streams_of[2], (ARMS,), 0, 2), jax.random.fold_in(streams_of[2], 1), 0, 1).astype(jnp.int32),
    }


coupling_full = 0.15
contour_step = 0.05
chi_value = 2.0
mixing = 0.5


def stencil(values, coupling):
    beside = jnp.roll(values, 1, 0) + jnp.roll(values, -1, 0)
    beside = beside + jnp.roll(values, 1, 1) + jnp.roll(values, -1, 1)
    beside = beside + jnp.roll(values, 1, 2) + jnp.roll(values, -1, 2)
    return (1.0 - 6.0 * coupling) * values + coupling * beside


def substep(values, factor, coupling):
    return factor * stencil(factor * values, coupling)


def extrapolate(values, half_factor, full_factor):
    halves = substep(substep(values, half_factor, coupling_full / 2), half_factor, coupling_full / 2)
    whole_step = substep(values, full_factor, coupling_full)
    return (4.0 * halves - whole_step) / 3.0


def factors(fields, arm_label):
    field_arm = jnp.where(arm_label == 0, fields[0], fields[1])
    return jnp.exp(-field_arm * (contour_step / 4)), jnp.exp(-field_arm * (contour_step / 2))


def reference(fields, starts, labels):
    def forward(inputs):
        arm_label, initial = inputs
        half_factor, full_factor = factors(fields, arm_label)
        step_one = extrapolate(initial, half_factor, full_factor)
        step_two = extrapolate(step_one, half_factor, full_factor)
        return step_one, step_two

    step_ones, step_twos = lax.map(forward, (labels, starts))
    junction = jnp.prod(step_twos, axis=0)
    partition = jnp.mean(junction)

    def backward(inputs):
        arm_label, step_one, step_two = inputs
        half_factor, full_factor = factors(fields, arm_label)
        back_one = extrapolate(junction / step_two, half_factor, full_factor)
        back_two = extrapolate(back_one, half_factor, full_factor)
        segment = 0.25 * back_two + 0.5 * step_one * back_one + 0.25 * junction
        return segment / (ARMS * partition)

    segments = lax.map(backward, (labels, step_ones, step_twos))
    is_type_a = (labels == 0)[:, None, None, None]
    dens_a = jnp.sum(jnp.where(is_type_a, segments, 0.0), axis=0)
    dens_b = jnp.sum(jnp.where(is_type_a, 0.0, segments), axis=0)
    density = jnp.stack([dens_a, dens_b])
    pressure = 0.5 * (fields[0] + fields[1] - chi_value)
    update_a = fields[0] + mixing * (chi_value * dens_b + pressure - fields[0])
    update_b = fields[1] + mixing * (chi_value * dens_a + pressure - fields[1])
    return density, jnp.stack([update_a, update_b])
```

```python
import jax
import jax.numpy as jnp
from jax import lax
from jax.experimental import pallas as pl
from jax.experimental.pallas import tpu as pltpu
from jax.sharding import PartitionSpec as P

coupling_full = 0.15
contour_step = 0.05
chi_value = 2.0
mixing = 0.5
ARMS, NX, NY, NZ = 16, 256, 64, 128
MESH = pl.DeviceIdType.MESH


def stencil(ref, p, c):
    m = ref[p]
    s = ref[p - 1] + ref[p + 1]
    s = s + (pltpu.roll(m, 1, 0) + pltpu.roll(m, NY - 1, 0))
    s = s + (pltpu.roll(m, 1, 1) + pltpu.roll(m, NZ - 1, 1))
    return (1.0 - 6.0 * c) * m + c * s


def contour(value, hf, ff, base, count, u, w, u2, emit):
    def scale(p, _):
        v = value(p)
        u[p] = hf(base + p) * v
        w[p] = ff(base + p) * v
        return 0

    def first(p, _):
        u2[p] = ff(base + p) * stencil(u, p, coupling_full / 2)
        return 0

    def second(p, _):
        h = hf(base + p) * stencil(u2, p, coupling_full / 2)
        f = ff(base + p) * stencil(w, p, coupling_full)
        emit(p, (4.0 / 3.0) * h - (1.0 / 3.0) * f)
        return 0

    lax.fori_loop(0, count, scale, 0)
    lax.fori_loop(1, count - 1, first, 0)
    lax.fori_loop(2, count - 2, second, 0)


def kernel(
    fields, starts, labels, out, scale_out,
    fld, st, hf, ff, u, w, u2, step, f1s, rb, gs, pr, chip_in, jn, x_in, acc, d_in, zs, ys, xs,
    local_sem, fld_s, fld_r, st_s, st_r, rb_s, rb_r, g_s, g_r, pc_s, pc_r, px_s, px_r, j_s, j_r,
    d_s, d_r, z_s, z_r, y_s, y_r, x_s, x_r,
):
    me_a, me_s = lax.axis_index("arm"), lax.axis_index("space")
    up, dn = lax.rem(me_s + 1, 64), lax.rem(me_s + 63, 64)
    core, high = lax.rem(me_a, 2), me_a // 2
    chip = (high * 2 + 1 - core, me_s)
    across = ((1 - high) * 2 + core, me_s)
    cross = ((1 - high) * 2 + 1 - core, me_s)
    z = lax.rem(me_s, 8)
    row = me_s // 8
    y, x_lo = row // 2, lax.rem(row, 2)
    z_peer = [(me_a, me_s - z + lax.rem(z + k, 8)) for k in range(1, 8)]
    y_peer = [(me_a, me_s + (lax.rem(y + k, 4) - y) * 16) for k in range(1, 4)]
    x_peer = (me_a, me_s + 8 - 16 * x_lo)
    sides = [(me_a, up), (me_a, dn)]

    def send(src, dst, ss, rs, to):
        return pltpu.make_async_remote_copy(src, dst, ss, rs, device_id=to, device_id_type=MESH)

    own_f = pltpu.make_async_copy(fields, fld.at[:, pl.ds(4, 4)], local_sem.at[4])
    own_f.start()
    own = [pltpu.make_async_copy(starts.at[a], st.at[a, pl.ds(4, 4)], local_sem.at[a]) for a in range(4)]
    for c in own:
        c.start()

    barrier = pltpu.get_barrier_semaphore()
    peers = sides + [chip, across, cross] + z_peer + y_peer + [x_peer]
    for to in peers:
        pl.semaphore_signal(barrier, inc=1, device_id=to, device_id_type=MESH)
    pl.semaphore_wait(barrier, len(peers))

    own_f.wait()
    fld_c = [
        send(fld.at[:, pl.ds(4, 4)], fld.at[:, pl.ds(8 * i, 4)], fld_s.at[i], fld_r.at[i], sides[i])
        for i in range(2)
    ]
    for c in fld_c:
        c.start()
    st_c = []
    for a in range(4):
        own[a].wait()
        for i in range(2):
            c = send(
                st.at[a, pl.ds(4, 4)], st.at[a, pl.ds(8 * i, 4)], st_s.at[a, i], st_r.at[a, i], sides[i]
            )
            c.start()
            st_c.append(c)
    for c in fld_c:
        c.wait_recv()

    def factor(p, _):
        for t in range(2):
            h = jnp.exp(fld[t, p] * (-contour_step / 4))
            hf[t, p] = h
            ff[t, p] = h * h
        return 0

    lax.fori_loop(0, 12, factor, 0)

    rb_c = []
    for a in range(4):
        lab = labels[a]
        is_a = lab == 0
        for c in st_c[2 * a : 2 * a + 2]:
            c.wait_recv()

        def keep_one(p, v):
            step[p] = v

        contour(lambda p: st[a, p], lambda p: hf[lab, p], lambda p: ff[lab, p], 0, 12, u, w, u2, keep_one)

        def keep_two(p, v):
            own_p = p - 2
            f1s[a, own_p] = step[p + 2]
            r = 1.0 / v
            rb[a, p] = r
            ra = jnp.where(is_a, r, 0.0)
            rz = jnp.where(is_a, 0.0, r)
            if a == 0:
                pr[own_p] = v
                gs[0, p + 2] = ra
                gs[1, p + 2] = rz
            else:
                pr[own_p] = pr[own_p] * v
                gs[0, p + 2] = gs[0, p + 2] + ra
                gs[1, p + 2] = gs[1, p + 2] + rz

        contour(
            lambda p: step[p + 2], lambda p: hf[lab, p], lambda p: ff[lab, p], 2, 8, u, w, u2, keep_two
        )
        for i in range(2):
            c = send(
                rb.at[a, pl.ds(4 - 2 * i, 2)], rb.at[a, pl.ds(6 * i, 2)], rb_s.at[a, i], rb_r.at[a, i], sides[i]
            )
            if a == 3 and i == 0:
                pc = send(pr, chip_in, pc_s, pc_r, chip)
                pc.start()
            c.start()
            rb_c.append(c)

    g_c = [
        send(gs.at[:, pl.ds(4 + 2 * i, 2)], gs.at[:, pl.ds(10 * i, 2)], g_s.at[i], g_r.at[i], sides[i])
        for i in range(2)
    ]
    for c in g_c:
        c.start()

    pc.wait_recv()
    pc.wait_send()
    for p in range(4):
        pr[p] = pr[p] * chip_in[p]
    half = pl.ds(2 * core, 2)
    px = [
        send(pr.at[half], x_in.at[half], px_s.at[0], px_r.at[0], across),
        send(pr.at[half], x_in.at[half], px_s.at[1], px_r.at[1], cross),
    ]
    for c in px:
        c.start()
    for c in px:
        c.wait_recv()
    total = jnp.zeros((8, NZ), jnp.float32)
    for p in range(4):
        j = pr[p] * x_in[p]
        jn[4 + p] = j
        for q in range(8):
            total = total + j[8 * q : 8 * q + 8]
    j_c = [
        send(jn.at[pl.ds(4, 4)], jn.at[pl.ds(8 * i, 4)], j_s.at[i], j_r.at[i], sides[i]) for i in range(2)
    ]
    for c in j_c:
        c.start()
    zs[0] = total
    z_c = [send(zs.at[0], zs.at[k + 1], z_s.at[k], z_r.at[k], z_peer[k]) for k in range(7)]
    for c in z_c:
        c.start()

    for c in rb_c:
        c.wait_recv()
    for a in range(4):
        is_a = labels[a] == 0
        for p in (0, 1, 6, 7):
            r = rb[a, p]
            ra = jnp.where(is_a, r, 0.0)
            rz = jnp.where(is_a, 0.0, r)
            if a == 0:
                gs[0, p + 2] = ra
                gs[1, p + 2] = rz
            else:
                gs[0, p + 2] = gs[0, p + 2] + ra
                gs[1, p + 2] = gs[1, p + 2] + rz

    count_a = jnp.float32(0.0)
    for a in range(4):
        count_a = count_a + jnp.where(labels[a] == 0, 1.0, 0.0)

    def add(t, p, v):
        for b in range(4):
            acc[b, t, p] = acc[b, t, p] + v[16 * b : 16 * b + 16]

    for p in range(4):
        j = 0.25 * jn[4 + p]
        for b in range(4):
            acc[b, 0, p] = count_a * j[16 * b : 16 * b + 16]
            acc[b, 1, p] = (4.0 - count_a) * j[16 * b : 16 * b + 16]

    for c in j_c:
        c.wait_recv()

    for a in range(4):
        lab = labels[a]
        is_a = lab == 0

        def middle(p, v):
            v = 0.5 * f1s[a, p - 2] * v
            add(0, p - 2, jnp.where(is_a, v, 0.0))
            add(1, p - 2, jnp.where(is_a, 0.0, v))

        contour(
            lambda p: jn[p + 2] * rb[a, p], lambda p: hf[lab, p], lambda p: ff[lab, p], 2, 8, u, w, u2, middle
        )
        if a == 1:
            for c in z_c:
                c.wait_recv()
            s = zs[0]
            for k in range(1, 8):
                s = s + zs[k]
            ys[0] = s
            y_c = [send(ys.at[0], ys.at[k + 1], y_s.at[k], y_r.at[k], y_peer[k]) for k in range(3)]
            for c in y_c:
                c.start()

    for c in g_c:
        c.wait_recv()
    for t in range(2):
        def keep_one(p, v):
            step[p] = v

        contour(lambda p: jn[p] * gs[t, p], lambda p: hf[t, p], lambda p: ff[t, p], 0, 12, u, w, u2, keep_one)

        if t == 0:
            for c in y_c:
                c.wait_recv()
            s = (ys[0] + ys[1]) + (ys[2] + ys[3])
            xs[0] = s
            x_c = send(xs.at[0], xs.at[1], x_s, x_r, x_peer)
            x_c.start()

        def last(p, v):
            add(t, p - 2, 0.25 * v)

        contour(lambda p: step[p + 2], lambda p: hf[t, p], lambda p: ff[t, p], 2, 8, u, w, u2, last)

    owners = [across, cross, chip]
    d_c = [
        send(acc.at[to[0]], d_in.at[k], d_s.at[k], d_r.at[k], to) for k, to in enumerate(owners)
    ]
    for c in d_c:
        c.start()
    x_c.wait_recv()
    s = jnp.sum(jnp.sum(xs[0] + xs[1], axis=0, keepdims=True), axis=1, keepdims=True)
    cells = float(NX * NY * NZ)
    scale_out[...] = jnp.broadcast_to(1.0 / (ARMS * (s / cells)), (8, NZ))
    for c in d_c:
        c.wait_recv()
    for t in range(2):
        for p in range(4):
            out[t, p] = (acc[me_a, t, p] + d_in[2, t, p]) + (d_in[0, t, p] + d_in[1, t, p])
    for c in fld_c + st_c + rb_c + g_c + px + j_c + z_c + y_c + [x_c] + d_c:
        c.wait_send()


def local(fields, starts, labels):
    vmem = lambda *shape: pltpu.VMEM(shape, jnp.float32)
    dma = lambda *shape: pltpu.SemaphoreType.DMA(shape)
    plane = (NY, NZ)
    total, scale = pl.pallas_call(
        kernel,
        out_shape=(
            jax.ShapeDtypeStruct((2, 4, 16, NZ), jnp.float32),
            jax.ShapeDtypeStruct((8, NZ), jnp.float32),
        ),
        in_specs=[
            pl.BlockSpec(memory_space=pl.ANY),
            pl.BlockSpec(memory_space=pl.ANY),
            pl.BlockSpec(memory_space=pltpu.SMEM),
        ],
        out_specs=(pl.BlockSpec(memory_space=pltpu.VMEM), pl.BlockSpec(memory_space=pltpu.VMEM)),
        scratch_shapes=[
            vmem(2, 12, *plane), vmem(4, 12, *plane), vmem(2, 12, *plane), vmem(2, 12, *plane),
            vmem(12, *plane), vmem(12, *plane), vmem(12, *plane), vmem(12, *plane),
            vmem(4, 4, *plane), vmem(4, 8, *plane), vmem(2, 12, *plane),
            vmem(4, *plane), vmem(4, *plane), vmem(12, *plane), vmem(4, *plane),
            vmem(4, 2, 4, 16, NZ), vmem(3, 2, 4, 16, NZ),
            vmem(8, 8, NZ), vmem(4, 8, NZ), vmem(2, 8, NZ),
            dma(5), dma(2), dma(2), dma(4, 2), dma(4, 2), dma(4, 2), dma(4, 2), dma(2), dma(2),
            pltpu.SemaphoreType.DMA, pltpu.SemaphoreType.DMA, dma(2), dma(2), dma(2), dma(2),
            dma(3), dma(3), dma(7), dma(7), dma(3), dma(3), pltpu.SemaphoreType.DMA, pltpu.SemaphoreType.DMA,
        ],
        compiler_params=pltpu.CompilerParams(collective_id=0, has_side_effects=True),
    )(fields, starts, labels)
    density = total * scale[0, 0]
    owned = lax.dynamic_slice_in_dim(fields, lax.axis_index("arm") * 16, 16, 2)
    pressure = 0.5 * (owned[0] + owned[1] - chi_value)
    update_a = owned[0] + mixing * (chi_value * density[1] + pressure - owned[0])
    update_b = owned[1] + mixing * (chi_value * density[0] + pressure - owned[1])
    return density, jnp.stack([update_a, update_b])


def solution(mesh):
    in_specs = (P(None, "space", None, None), P("arm", "space", None, None), P("arm"))
    out_specs = (P(None, "space", "arm", None), P(None, "space", "arm", None))
    return jax.shard_map(local, mesh=mesh, in_specs=in_specs, out_specs=out_specs, check_vma=False)
```

```python
import jax
import jax.numpy as jnp
from jax import lax
from jax.experimental import pallas as pl
from jax.experimental.pallas import tpu as pltpu
from jax.sharding import PartitionSpec as P

coupling_full = 0.15
contour_step = 0.05
chi_value = 2.0
mixing = 0.5
ARMS, NX, NY, NZ = 16, 256, 64, 128
MESH = pl.DeviceIdType.MESH


def stencil(ref, p, c):
    m = ref[p]
    s = ref[p - 1] + ref[p + 1]
    s = s + (pltpu.roll(m, 1, 0) + pltpu.roll(m, NY - 1, 0))
    s = s + (pltpu.roll(m, 1, 1) + pltpu.roll(m, NZ - 1, 1))
    return (1.0 - 6.0 * c) * m + c * s


def contour(value, hf, ff, base, count, u, w, u2, emit):
    for p in range(count):
        v = value(p)
        u[p] = hf(base + p) * v
        w[p] = ff(base + p) * v
    for p in range(1, count - 1):
        u2[p] = ff(base + p) * stencil(u, p, coupling_full / 2)
    for p in range(2, count - 2):
        h = hf(base + p) * stencil(u2, p, coupling_full / 2)
        f = ff(base + p) * stencil(w, p, coupling_full)
        emit(p, (4.0 / 3.0) * h - (1.0 / 3.0) * f)


def kernel(
    fields, starts, labels, density, new_fields,
    fld, st, hf, ff, u, w, u2, step, f1s, rb, gs, pr, chip_in, jn, x_in, acc, d_in, zs, ys, xs,
    local_sem, fld_s, fld_r, st_s, st_r, rb_s, rb_r, g_s, g_r, pc_s, pc_r, px_s, px_r, j_s, j_r,
    d_s, d_r, z_s, z_r, y_s, y_r, x_s, x_r,
):
    me_a, me_s = lax.axis_index("arm"), lax.axis_index("space")
    up, dn = lax.rem(me_s + 1, 64), lax.rem(me_s + 63, 64)
    core, high = lax.rem(me_a, 2), me_a // 2
    chip = (high * 2 + 1 - core, me_s)
    across = ((1 - high) * 2 + core, me_s)
    cross = ((1 - high) * 2 + 1 - core, me_s)
    z = lax.rem(me_s, 8)
    row = me_s // 8
    y, x_lo = row // 2, lax.rem(row, 2)
    z_peer = [(me_a, me_s - z + lax.rem(z + k, 8)) for k in range(1, 8)]
    y_peer = [(me_a, me_s + (lax.rem(y + k, 4) - y) * 16) for k in range(1, 4)]
    x_peer = (me_a, me_s + 8 - 16 * x_lo)
    sides = [(me_a, up), (me_a, dn)]

    def send(src, dst, ss, rs, to):
        return pltpu.make_async_remote_copy(src, dst, ss, rs, device_id=to, device_id_type=MESH)

    own_f = pltpu.make_async_copy(fields, fld.at[:, pl.ds(4, 4)], local_sem.at[4])
    own_f.start()
    own = [pltpu.make_async_copy(starts.at[a], st.at[a, pl.ds(4, 4)], local_sem.at[a]) for a in range(4)]
    for c in own:
        c.start()

    barrier = pltpu.get_barrier_semaphore()
    peers = sides + [chip, across, cross] + z_peer + y_peer + [x_peer]
    for to in peers:
        pl.semaphore_signal(barrier, inc=1, device_id=to, device_id_type=MESH)
    pl.semaphore_wait(barrier, len(peers))

    own_f.wait()
    fld_c = [
        send(fld.at[:, pl.ds(4, 4)], fld.at[:, pl.ds(8 * i, 4)], fld_s.at[i], fld_r.at[i], sides[i])
        for i in range(2)
    ]
    for c in fld_c:
        c.start()

    def start_copy(a, i):
        return send(st.at[a, pl.ds(4, 4)], st.at[a, pl.ds(8 * i, 4)], st_s.at[a, i], st_r.at[a, i], sides[i])

    def end_copy(a, i):
        return send(
            rb.at[a, pl.ds(4 - 2 * i, 2)], rb.at[a, pl.ds(6 * i, 2)], rb_s.at[a, i], rb_r.at[a, i], sides[i]
        )

    for a in range(4):
        own[a].wait()
        for i in range(2):
            start_copy(a, i).start()
    pr[...] = jnp.ones_like(pr)
    gs[:, 2:10] = jnp.zeros((2, 8, NY, NZ), jnp.float32)
    for c in fld_c:
        c.wait_recv()

    def factor(p, _):
        for t in range(2):
            h = jnp.exp(fld[t, p] * (-contour_step / 4))
            hf[t, p] = h
            ff[t, p] = h * h
        return 0

    lax.fori_loop(0, 12, factor, 0)

    def forward(a, _):
        lab = labels[a]
        is_a = lab == 0
        for i in range(2):
            start_copy(a, i).wait_recv()

        def keep_one(p, v):
            step[p] = v

        contour(lambda p: st[a, p], lambda p: hf[lab, p], lambda p: ff[lab, p], 0, 12, u, w, u2, keep_one)

        def keep_two(p, v):
            own_p = p - 2
            f1s[a, own_p] = step[p + 2]
            r = 1.0 / v
            rb[a, p] = r
            pr[own_p] = pr[own_p] * v
            gs[0, p + 2] = gs[0, p + 2] + jnp.where(is_a, r, 0.0)
            gs[1, p + 2] = gs[1, p + 2] + jnp.where(is_a, 0.0, r)

        contour(
            lambda p: step[p + 2], lambda p: hf[lab, p], lambda p: ff[lab, p], 2, 8, u, w, u2, keep_two
        )
        for i in range(2):
            end_copy(a, i).start()
        return 0

    lax.fori_loop(0, 4, forward, 0)
    pc = send(pr, chip_in, pc_s, pc_r, chip)
    pc.start()
    g_c = [
        send(gs.at[:, pl.ds(4 + 2 * i, 2)], gs.at[:, pl.ds(10 * i, 2)], g_s.at[i], g_r.at[i], sides[i])
        for i in range(2)
    ]
    for c in g_c:
        c.start()

    pc.wait_recv()
    pc.wait_send()
    for p in range(4):
        pr[p] = pr[p] * chip_in[p]
    half = pl.ds(2 * core, 2)
    px = [
        send(pr.at[half], x_in.at[half], px_s.at[0], px_r.at[0], across),
        send(pr.at[half], x_in.at[half], px_s.at[1], px_r.at[1], cross),
    ]
    for c in px:
        c.start()
    for c in px:
        c.wait_recv()
    total = jnp.zeros((8, NZ), jnp.float32)
    for p in range(4):
        j = pr[p] * x_in[p]
        jn[4 + p] = j
        for q in range(8):
            total = total + j[8 * q : 8 * q + 8]
    j_c = [
        send(jn.at[pl.ds(4, 4)], jn.at[pl.ds(8 * i, 4)], j_s.at[i], j_r.at[i], sides[i]) for i in range(2)
    ]
    for c in j_c:
        c.start()
    zs[0] = total
    z_c = [send(zs.at[0], zs.at[k + 1], z_s.at[k], z_r.at[k], z_peer[k]) for k in range(7)]
    for c in z_c:
        c.start()

    for a in range(4):
        is_a = labels[a] == 0
        for i in range(2):
            end_copy(a, i).wait_recv()
        for p in (0, 1, 6, 7):
            r = rb[a, p]
            gs[0, p + 2] = gs[0, p + 2] + jnp.where(is_a, r, 0.0)
            gs[1, p + 2] = gs[1, p + 2] + jnp.where(is_a, 0.0, r)

    count_a = jnp.float32(0.0)
    for a in range(4):
        count_a = count_a + jnp.where(labels[a] == 0, 1.0, 0.0)

    def add(t, p, v):
        for b in range(4):
            acc[b, t, p] = acc[b, t, p] + v[16 * b : 16 * b + 16]

    for p in range(4):
        j = 0.25 * jn[4 + p]
        for b in range(4):
            acc[b, 0, p] = count_a * j[16 * b : 16 * b + 16]
            acc[b, 1, p] = (4.0 - count_a) * j[16 * b : 16 * b + 16]

    for c in j_c:
        c.wait_recv()

    def backward(a, _):
        lab = labels[a]
        is_a = lab == 0

        def middle(p, v):
            v = 0.5 * f1s[a, p - 2] * v
            add(0, p - 2, jnp.where(is_a, v, 0.0))
            add(1, p - 2, jnp.where(is_a, 0.0, v))

        contour(
            lambda p: jn[p + 2] * rb[a, p], lambda p: hf[lab, p], lambda p: ff[lab, p], 2, 8, u, w, u2, middle
        )
        return 0

    lax.fori_loop(0, 4, backward, 0)
    for c in z_c:
        c.wait_recv()
    s = zs[0]
    for k in range(1, 8):
        s = s + zs[k]
    ys[0] = s
    y_c = [send(ys.at[0], ys.at[k + 1], y_s.at[k], y_r.at[k], y_peer[k]) for k in range(3)]
    for c in y_c:
        c.start()
    for c in g_c:
        c.wait_recv()

    def both(t, _):
        def keep_one(p, v):
            step[p] = v

        contour(lambda p: jn[p] * gs[t, p], lambda p: hf[t, p], lambda p: ff[t, p], 0, 12, u, w, u2, keep_one)

        def last(p, v):
            add(t, p - 2, 0.25 * v)

        contour(lambda p: step[p + 2], lambda p: hf[t, p], lambda p: ff[t, p], 2, 8, u, w, u2, last)
        return 0

    lax.fori_loop(0, 2, both, 0)
    owners = [across, cross, chip]
    d_c = [
        send(acc.at[to[0]], d_in.at[k], d_s.at[k], d_r.at[k], to) for k, to in enumerate(owners)
    ]
    for c in d_c:
        c.start()
    for c in y_c:
        c.wait_recv()
    xs[0] = (ys[0] + ys[1]) + (ys[2] + ys[3])
    x_c = send(xs.at[0], xs.at[1], x_s, x_r, x_peer)
    x_c.start()
    x_c.wait_recv()
    s = jnp.sum(jnp.sum(xs[0] + xs[1], axis=0, keepdims=True), axis=1, keepdims=True)
    cells = float(NX * NY * NZ)
    scale = jnp.broadcast_to(1.0 / (ARMS * (s / cells)), (16, NZ))
    rows = pl.ds(pl.multiple_of(16 * me_a, 16), 16)
    for c in d_c:
        c.wait_recv()
    for p in range(4):
        d = [
            scale * ((acc[me_a, t, p] + d_in[2, t, p]) + (d_in[0, t, p] + d_in[1, t, p])) for t in range(2)
        ]
        f = [fld[t, 4 + p, rows] for t in range(2)]
        pressure = 0.5 * (f[0] + f[1] - chi_value)
        for t in range(2):
            density[t, p] = d[t]
            new_fields[t, p] = f[t] + mixing * (chi_value * d[1 - t] + pressure - f[t])
    for a in range(4):
        for i in range(2):
            start_copy(a, i).wait_send()
            end_copy(a, i).wait_send()
    for c in fld_c + g_c + px + j_c + z_c + y_c + [x_c] + d_c:
        c.wait_send()


def local(fields, starts, labels):
    vmem = lambda *shape: pltpu.VMEM(shape, jnp.float32)
    dma = lambda *shape: pltpu.SemaphoreType.DMA(shape)
    plane = (NY, NZ)
    return pl.pallas_call(
        kernel,
        out_shape=(jax.ShapeDtypeStruct((2, 4, 16, NZ), jnp.float32),) * 2,
        in_specs=[
            pl.BlockSpec(memory_space=pl.ANY),
            pl.BlockSpec(memory_space=pl.ANY),
            pl.BlockSpec(memory_space=pltpu.SMEM),
        ],
        out_specs=(pl.BlockSpec(memory_space=pltpu.VMEM), pl.BlockSpec(memory_space=pltpu.VMEM)),
        scratch_shapes=[
            vmem(2, 12, *plane), vmem(4, 12, *plane), vmem(2, 12, *plane), vmem(2, 12, *plane),
            vmem(12, *plane), vmem(12, *plane), vmem(12, *plane), vmem(12, *plane),
            vmem(4, 4, *plane), vmem(4, 8, *plane), vmem(2, 12, *plane),
            vmem(4, *plane), vmem(4, *plane), vmem(12, *plane), vmem(4, *plane),
            vmem(4, 2, 4, 16, NZ), vmem(3, 2, 4, 16, NZ),
            vmem(8, 8, NZ), vmem(4, 8, NZ), vmem(2, 8, NZ),
            dma(5), dma(2), dma(2), dma(4, 2), dma(4, 2), dma(4, 2), dma(4, 2), dma(2), dma(2),
            pltpu.SemaphoreType.DMA, pltpu.SemaphoreType.DMA, dma(2), dma(2), dma(2), dma(2),
            dma(3), dma(3), dma(7), dma(7), dma(3), dma(3), pltpu.SemaphoreType.DMA, pltpu.SemaphoreType.DMA,
        ],
        compiler_params=pltpu.CompilerParams(collective_id=0, has_side_effects=True),
    )(fields, starts, labels)


def solution(mesh):
    in_specs = (P(None, "space", None, None), P("arm", "space", None, None), P("arm"))
    out_specs = (P(None, "space", "arm", None), P(None, "space", "arm", None))
    return jax.shard_map(local, mesh=mesh, in_specs=in_specs, out_specs=out_specs, check_vma=False)
```

```python
import jax
import jax.numpy as jnp
from jax import lax
from jax.experimental import pallas as pl
from jax.experimental.pallas import tpu as pltpu
from jax.sharding import PartitionSpec as P

coupling_full = 0.15
contour_step = 0.05
chi_value = 2.0
mixing = 0.5
ARMS, NX, NY, NZ = 16, 256, 64, 128
MESH = pl.DeviceIdType.MESH


def stencil(ref, p, c):
    m = ref[p]
    s = ref[p - 1] + ref[p + 1]
    s = s + (pltpu.roll(m, 1, 0) + pltpu.roll(m, NY - 1, 0))
    s = s + (pltpu.roll(m, 1, 1) + pltpu.roll(m, NZ - 1, 1))
    return (1.0 - 6.0 * c) * m + c * s


def contour(value, hf, ff, base, count, u, w, u2, emit):
    for p in range(count):
        v = value(p)
        u[p] = hf(base + p) * v
        w[p] = ff(base + p) * v
    for p in range(1, count - 1):
        u2[p] = ff(base + p) * stencil(u, p, coupling_full / 2)
    for p in range(2, count - 2):
        h = hf(base + p) * stencil(u2, p, coupling_full / 2)
        f = ff(base + p) * stencil(w, p, coupling_full)
        emit(p, (4.0 / 3.0) * h - (1.0 / 3.0) * f)


def kernel(
    fields, starts, labels, density, new_fields,
    fld, st, hf, ff, u, w, u2, step, f1s, rb, gs, g_in, gc, pr, chip_in, p2, x_in, jn, acc, d_in, zs, ys, xs,
    local_sem, fld_s, fld_r, fc_s, fc_r, st_s, st_r, rb_s, rb_r, gi_s, gi_r, g_s, g_r, pc_s, pc_r, px_s, px_r,
    j_s, j_r, d_s, d_r, z_s, z_r, y_s, y_r, x_s, x_r, near_z, far_z, near_y,
):
    me_a, me_s = lax.axis_index("arm"), lax.axis_index("space")
    up, dn = lax.rem(me_s + 1, 64), lax.rem(me_s + 63, 64)
    core, high = lax.rem(me_a, 2), me_a // 2
    arm_c = high * 2 + 1 - core
    chip = (arm_c, me_s)
    across = ((1 - high) * 2 + core, me_s)
    cross = ((1 - high) * 2 + 1 - core, me_s)
    z = lax.rem(me_s, 8)
    row = me_s // 8
    y, x_lo = row // 2, lax.rem(row, 2)
    z_peer = [(me_a, me_s - z + lax.rem(z + k, 8)) for k in range(1, 8)]
    y_peer = [(me_a, me_s + (lax.rem(y + k, 4) - y) * 16) for k in range(1, 4)]
    x_s_id = me_s + 8 - 16 * x_lo
    x_peer = [(me_a, x_s_id), (arm_c, me_s), (arm_c, x_s_id)]
    sides = [(me_a, up), (me_a, dn)]
    cross_sides = [(arm_c, up), (arm_c, dn)]

    def send(src, dst, ss, rs, to):
        return pltpu.make_async_remote_copy(src, dst, ss, rs, device_id=to, device_id_type=MESH)

    def signal(sem, to):
        pl.semaphore_signal(sem, inc=1, device_id=to, device_id_type=MESH)

    own_f = pltpu.make_async_copy(fields, fld.at[:, pl.ds(4, 4)], local_sem.at[4])
    own_f.start()
    own = [pltpu.make_async_copy(starts.at[a], st.at[a, pl.ds(4, 4)], local_sem.at[a]) for a in range(4)]
    for c in own:
        c.start()

    barrier = pltpu.get_barrier_semaphore()
    near = [z_peer[0], z_peer[6]]
    peers = sides + cross_sides + [chip, across, cross] + near + [y_peer[0], y_peer[2], x_peer[0], x_peer[2]]
    for to in peers:
        signal(barrier, to)
    pl.semaphore_wait(barrier, len(peers))

    own_f.wait()
    fld_c = [
        send(fld.at[core, pl.ds(4, 4)], fld.at[core, pl.ds(8 * i, 4)], fld_s.at[i], fld_r.at[i], sides[i])
        for i in range(2)
    ]
    for c in fld_c:
        c.start()

    def start_copy(a, i):
        return send(st.at[a, pl.ds(4, 4)], st.at[a, pl.ds(8 * i, 4)], st_s.at[a, i], st_r.at[a, i], sides[i])

    def end_copy(a, i):
        return send(
            rb.at[a, pl.ds(4 - 2 * i, 2)], rb.at[a, pl.ds(6 * i, 2)], rb_s.at[a, i], rb_r.at[a, i], sides[i]
        )

    for a in range(4):
        own[a].wait()
        for i in range(2):
            start_copy(a, i).start()
    for to in near:
        signal(near_z, to)
    for k in (0, 2):
        signal(near_y, y_peer[k])
    pr[...] = jnp.ones_like(pr)
    gs[...] = jnp.zeros_like(gs)
    fc_c = [
        send(fld.at[core, pl.ds(8 * i, 4)], fld.at[core, pl.ds(8 * i, 4)], fc_s.at[i], fc_r.at[i], chip)
        for i in range(2)
    ]
    for i in range(2):
        fld_c[i].wait_recv()
        fc_c[i].start()

    pl.semaphore_wait(near_z, 2)
    for k in (1, 5):
        signal(far_z, z_peer[k])
    for c in fc_c:
        c.wait_recv()

    def factor(p, _):
        for t in range(2):
            h = jnp.exp(fld[t, p] * (-contour_step / 4))
            hf[t, p] = h
            ff[t, p] = h * h
        return 0

    lax.fori_loop(0, 12, factor, 0)

    def forward(a, _):
        lab = labels[a]
        is_a = lab == 0
        for i in range(2):
            start_copy(a, i).wait_recv()

        def keep_one(p, v):
            step[p] = v

        contour(lambda p: st[a, p], lambda p: hf[lab, p], lambda p: ff[lab, p], 0, 12, u, w, u2, keep_one)

        def keep_two(p, v):
            own_p = p - 2
            f1s[a, own_p] = step[p + 2]
            r = 1.0 / v
            rb[a, p] = r
            pr[own_p] = pr[own_p] * v
            gs[0, own_p] = gs[0, own_p] + jnp.where(is_a, r, 0.0)
            gs[1, own_p] = gs[1, own_p] + jnp.where(is_a, 0.0, r)

        contour(
            lambda p: step[p + 2], lambda p: hf[lab, p], lambda p: ff[lab, p], 2, 8, u, w, u2, keep_two
        )
        for i in range(2):
            end_copy(a, i).start()
        return 0

    lax.fori_loop(0, 4, forward, 0)

    mine = 2 * core
    pc = send(pr.at[pl.ds(2 - mine, 2)], chip_in, pc_s, pc_r, chip)
    pc.start()
    gi = send(gs.at[1 - core], g_in, gi_s, gi_r, chip)
    gi.start()
    pc.wait_recv()
    for k in range(2):
        p2[k] = pr[mine + k] * chip_in[k]
    px = send(p2, x_in, px_s, px_r, across)
    px.start()
    gi.wait_recv()
    for p in range(4):
        gc[4 + p] = gs[core, p] + g_in[p]
    g_c = [
        send(gc.at[pl.ds(4, 4)], gc.at[pl.ds(8 * i, 4)], g_s.at[i], g_r.at[i], sides[i]) for i in range(2)
    ]
    for c in g_c:
        c.start()
    pl.semaphore_wait(far_z, 2)
    px.wait_recv()
    total = jnp.zeros((8, NZ), jnp.float32)
    for k in range(2):
        j = p2[k] * x_in[k]
        jn[4 + mine + k] = j
        for q in range(8):
            total = total + j[8 * q : 8 * q + 8]
    j_to = [(sides[0], 0), (cross_sides[0], 0), (sides[1], 8), (cross_sides[1], 8), (chip, 4)]
    j_c = [
        send(jn.at[pl.ds(4 + mine, 2)], jn.at[pl.ds(at + mine, 2)], j_s.at[i], j_r.at[i], to)
        for i, (to, at) in enumerate(j_to)
    ]
    for c in j_c:
        c.start()
    zs[0] = total
    z_c = [send(zs.at[0], zs.at[k + 1], z_s.at[k], z_r.at[k], z_peer[k]) for k in range(7)]
    for c in z_c:
        c.start()

    count_a = jnp.float32(0.0)
    for a in range(4):
        count_a = count_a + jnp.where(labels[a] == 0, 1.0, 0.0)

    def add(t, p, v):
        for b in range(4):
            acc[b, t, p] = acc[b, t, p] + v[16 * b : 16 * b + 16]

    j_c[4].wait_recv()
    for p in range(4):
        j = 0.25 * jn[4 + p]
        for b in range(4):
            acc[b, 0, p] = count_a * j[16 * b : 16 * b + 16]
            acc[b, 1, p] = (4.0 - count_a) * j[16 * b : 16 * b + 16]

    for a in range(4):
        for i in range(2):
            end_copy(a, i).wait_recv()
    for c in j_c[:4]:
        c.wait_recv()

    def backward(a, _):
        lab = labels[a]
        is_a = lab == 0

        def middle(p, v):
            v = 0.5 * f1s[a, p - 2] * v
            add(0, p - 2, jnp.where(is_a, v, 0.0))
            add(1, p - 2, jnp.where(is_a, 0.0, v))

        contour(
            lambda p: jn[p + 2] * rb[a, p], lambda p: hf[lab, p], lambda p: ff[lab, p], 2, 8, u, w, u2, middle
        )
        return 0

    lax.fori_loop(0, 4, backward, 0)
    for c in z_c:
        c.wait_recv()
    s = zs[0]
    for k in range(1, 8):
        s = s + zs[k]
    ys[0] = s
    pl.semaphore_wait(near_y, 2)
    y_c = [send(ys.at[0], ys.at[k + 1], y_s.at[k], y_r.at[k], y_peer[k]) for k in range(3)]
    for c in y_c:
        c.start()
    for c in g_c:
        c.wait_recv()

    def keep_back(p, v):
        step[p] = v

    contour(
        lambda p: jn[p] * gc[p], lambda p: hf[core, p], lambda p: ff[core, p], 0, 12, u, w, u2, keep_back
    )

    def last(p, v):
        add(core, p - 2, 0.25 * v)

    contour(lambda p: step[p + 2], lambda p: hf[core, p], lambda p: ff[core, p], 2, 8, u, w, u2, last)

    owners = [across, cross, chip]
    d_c = [send(acc.at[to[0]], d_in.at[k], d_s.at[k], d_r.at[k], to) for k, to in enumerate(owners)]
    for c in d_c:
        c.start()
    for c in y_c:
        c.wait_recv()
    xs[0] = (ys[0] + ys[1]) + (ys[2] + ys[3])
    x_c = [send(xs.at[0], xs.at[k + 1], x_s.at[k], x_r.at[k], x_peer[k]) for k in range(3)]
    for c in x_c:
        c.start()
    for c in x_c:
        c.wait_recv()
    s = (xs[0] + xs[1]) + (xs[2] + xs[3])
    s = jnp.sum(jnp.sum(s, axis=0, keepdims=True), axis=1, keepdims=True)
    cells = float(NX * NY * NZ)
    scale = jnp.broadcast_to(1.0 / (ARMS * (s / cells)), (16, NZ))
    rows = pl.ds(pl.multiple_of(16 * me_a, 16), 16)
    for c in d_c:
        c.wait_recv()
    for p in range(4):
        d = [
            scale * ((acc[me_a, t, p] + d_in[2, t, p]) + (d_in[0, t, p] + d_in[1, t, p])) for t in range(2)
        ]
        f = [fld[t, 4 + p, rows] for t in range(2)]
        pressure = 0.5 * (f[0] + f[1] - chi_value)
        for t in range(2):
            density[t, p] = d[t]
            new_fields[t, p] = f[t] + mixing * (chi_value * d[1 - t] + pressure - f[t])
    for a in range(4):
        for i in range(2):
            start_copy(a, i).wait_send()
            end_copy(a, i).wait_send()
    for c in fld_c + fc_c + [pc, gi, px] + g_c + j_c + z_c + y_c + x_c + d_c:
        c.wait_send()


def local(fields, starts, labels):
    vmem = lambda *shape: pltpu.VMEM(shape, jnp.float32)
    dma = lambda *shape: pltpu.SemaphoreType.DMA(shape)
    plane = (NY, NZ)
    return pl.pallas_call(
        kernel,
        out_shape=(jax.ShapeDtypeStruct((2, 4, 16, NZ), jnp.float32),) * 2,
        in_specs=[
            pl.BlockSpec(memory_space=pl.ANY),
            pl.BlockSpec(memory_space=pl.ANY),
            pl.BlockSpec(memory_space=pltpu.SMEM),
        ],
        out_specs=(pl.BlockSpec(memory_space=pltpu.VMEM), pl.BlockSpec(memory_space=pltpu.VMEM)),
        scratch_shapes=[
            vmem(2, 12, *plane), vmem(4, 12, *plane), vmem(2, 12, *plane), vmem(2, 12, *plane),
            vmem(12, *plane), vmem(12, *plane), vmem(12, *plane), vmem(12, *plane),
            vmem(4, 4, *plane), vmem(4, 8, *plane), vmem(2, 4, *plane), vmem(4, *plane), vmem(12, *plane),
            vmem(4, *plane), vmem(2, *plane), vmem(2, *plane), vmem(2, *plane), vmem(12, *plane),
            vmem(4, 2, 4, 16, NZ), vmem(3, 2, 4, 16, NZ),
            vmem(8, 8, NZ), vmem(4, 8, NZ), vmem(4, 8, NZ),
            dma(5), dma(2), dma(2), dma(2), dma(2), dma(4, 2), dma(4, 2), dma(4, 2), dma(4, 2),
            pltpu.SemaphoreType.DMA, pltpu.SemaphoreType.DMA, dma(2), dma(2),
            pltpu.SemaphoreType.DMA, pltpu.SemaphoreType.DMA, pltpu.SemaphoreType.DMA, pltpu.SemaphoreType.DMA,
            dma(5), dma(5), dma(3), dma(3), dma(7), dma(7), dma(3), dma(3), dma(3), dma(3),
            pltpu.SemaphoreType.REGULAR, pltpu.SemaphoreType.REGULAR, pltpu.SemaphoreType.REGULAR,
        ],
        compiler_params=pltpu.CompilerParams(collective_id=0, has_side_effects=True),
    )(fields, starts, labels)


def solution(mesh):
    in_specs = (P(None, "space", None, None), P("arm", "space", None, None), P("arm"))
    out_specs = (P(None, "space", "arm", None), P(None, "space", "arm", None))
    return jax.shard_map(local, mesh=mesh, in_specs=in_specs, out_specs=out_specs, check_vma=False)
```

```python
import jax
import jax.numpy as jnp
from jax import lax
from jax.experimental import pallas as pl
from jax.experimental.pallas import tpu as pltpu
from jax.sharding import PartitionSpec as P

coupling_full = 0.15
contour_step = 0.05
chi_value = 2.0
mixing = 0.5
ARMS, NX, NY, NZ = 16, 256, 64, 128
MESH = pl.DeviceIdType.MESH


def stencil(ref, p, c):
    m = ref[p]
    s = ref[p - 1] + ref[p + 1]
    s = s + (pltpu.roll(m, 1, 0) + pltpu.roll(m, NY - 1, 0))
    s = s + (pltpu.roll(m, 1, 1) + pltpu.roll(m, NZ - 1, 1))
    return (1.0 - 6.0 * c) * m + c * s


def contour(value, hf, ff, base, count, u, w, u2, emit):
    for p in range(count):
        v = value(p)
        u[p] = hf(base + p) * v
        w[p] = ff(base + p) * v
    for p in range(1, count - 1):
        u2[p] = ff(base + p) * stencil(u, p, coupling_full / 2)
    for p in range(2, count - 2):
        h = hf(base + p) * stencil(u2, p, coupling_full / 2)
        f = ff(base + p) * stencil(w, p, coupling_full)
        emit(p, (4.0 / 3.0) * h - (1.0 / 3.0) * f)


def kernel(
    fields, starts, labels_hbm, density, new_fields,
    labels, fld, st, hf, ff, u, w, u2, step, f1s, rb, gs, g_in, gc, pr, chip_in, p2, x_in, jn, acc, d_in, zs, ys, xs,
    local_sem, fld_s, fld_r, fc_s, fc_r, st_s, st_r, rb_s, rb_r, gi_s, gi_r, g_s, g_r, pc_s, pc_r, px_s, px_r,
    j_s, j_r, d_s, d_r, z_s, z_r, y_s, y_r, x_s, x_r, near_z, far_z, near_y,
):
    me_a, me_s = lax.axis_index("arm"), lax.axis_index("space")
    up, dn = lax.rem(me_s + 1, 64), lax.rem(me_s + 63, 64)
    core, high = lax.rem(me_a, 2), me_a // 2
    arm_c = high * 2 + 1 - core
    chip = (arm_c, me_s)
    across = ((1 - high) * 2 + core, me_s)
    cross = ((1 - high) * 2 + 1 - core, me_s)
    z = lax.rem(me_s, 8)
    row = me_s // 8
    y, x_lo = row // 2, lax.rem(row, 2)
    z_peer = [(me_a, me_s - z + lax.rem(z + k, 8)) for k in range(1, 8)]
    y_peer = [(me_a, me_s + (lax.rem(y + k, 4) - y) * 16) for k in range(1, 4)]
    x_s_id = me_s + 8 - 16 * x_lo
    x_peer = [(me_a, x_s_id), (arm_c, me_s), (arm_c, x_s_id)]
    sides = [(me_a, up), (me_a, dn)]
    cross_sides = [(arm_c, up), (arm_c, dn)]

    def send(src, dst, ss, rs, to):
        return pltpu.make_async_remote_copy(src, dst, ss, rs, device_id=to, device_id_type=MESH)

    def signal(sem, to):
        pl.semaphore_signal(sem, inc=1, device_id=to, device_id_type=MESH)

    own_l = pltpu.make_async_copy(labels_hbm, labels, local_sem.at[5])
    own_l.start()
    own_f = pltpu.make_async_copy(fields, fld.at[:, pl.ds(4, 4)], local_sem.at[4])
    own_f.start()
    own = [pltpu.make_async_copy(starts.at[a], st.at[a, pl.ds(4, 4)], local_sem.at[a]) for a in range(4)]
    for c in own:
        c.start()

    barrier = pltpu.get_barrier_semaphore()
    near = [z_peer[0], z_peer[6]]
    peers = sides + cross_sides + [chip, across, cross] + near + [y_peer[0], y_peer[2], x_peer[0], x_peer[2]]
    for to in peers:
        signal(barrier, to)
    pl.semaphore_wait(barrier, len(peers))

    own_l.wait()
    own_f.wait()
    fld_c = [
        send(fld.at[core, pl.ds(4, 4)], fld.at[core, pl.ds(8 * i, 4)], fld_s.at[i], fld_r.at[i], sides[i])
        for i in range(2)
    ]
    for c in fld_c:
        c.start()

    def start_copy(a, i):
        return send(st.at[a, pl.ds(4, 4)], st.at[a, pl.ds(8 * i, 4)], st_s.at[a, i], st_r.at[a, i], sides[i])

    def end_copy(a, i):
        return send(
            rb.at[a, pl.ds(4 - 2 * i, 2)], rb.at[a, pl.ds(6 * i, 2)], rb_s.at[a, i], rb_r.at[a, i], sides[i]
        )

    for a in range(4):
        own[a].wait()
        for i in range(2):
            start_copy(a, i).start()
    for to in near:
        signal(near_z, to)
    for k in (0, 2):
        signal(near_y, y_peer[k])
    pr[...] = jnp.ones_like(pr)
    gs[...] = jnp.zeros_like(gs)
    fc_c = [
        send(fld.at[core, pl.ds(8 * i, 4)], fld.at[core, pl.ds(8 * i, 4)], fc_s.at[i], fc_r.at[i], chip)
        for i in range(2)
    ]
    for i in range(2):
        fld_c[i].wait_recv()
        fc_c[i].start()

    pl.semaphore_wait(near_z, 2)
    for k in (1, 5):
        signal(far_z, z_peer[k])
    for c in fc_c:
        c.wait_recv()

    def factor(p, _):
        for t in range(2):
            h = jnp.exp(fld[t, p] * (-contour_step / 4))
            hf[t, p] = h
            ff[t, p] = h * h
        return 0

    lax.fori_loop(0, 12, factor, 0)

    def forward(a, _):
        lab = labels[a]
        is_a = lab == 0
        for i in range(2):
            start_copy(a, i).wait_recv()

        def keep_one(p, v):
            step[p] = v

        contour(lambda p: st[a, p], lambda p: hf[lab, p], lambda p: ff[lab, p], 0, 12, u, w, u2, keep_one)

        def keep_two(p, v):
            own_p = p - 2
            f1s[a, own_p] = step[p + 2]
            r = 1.0 / v
            rb[a, p] = r
            pr[own_p] = pr[own_p] * v
            gs[0, own_p] = gs[0, own_p] + jnp.where(is_a, r, 0.0)
            gs[1, own_p] = gs[1, own_p] + jnp.where(is_a, 0.0, r)

        contour(
            lambda p: step[p + 2], lambda p: hf[lab, p], lambda p: ff[lab, p], 2, 8, u, w, u2, keep_two
        )
        for i in range(2):
            end_copy(a, i).start()
        return 0

    lax.fori_loop(0, 4, forward, 0)

    mine = 2 * core
    pc = send(pr.at[pl.ds(2 - mine, 2)], chip_in, pc_s, pc_r, chip)
    pc.start()
    gi = send(gs.at[1 - core], g_in, gi_s, gi_r, chip)
    gi.start()
    pc.wait_recv()
    for k in range(2):
        p2[k] = pr[mine + k] * chip_in[k]
    px = send(p2, x_in, px_s, px_r, across)
    px.start()
    gi.wait_recv()
    for p in range(4):
        gc[4 + p] = gs[core, p] + g_in[p]
    pl.semaphore_wait(far_z, 2)
    px.wait_recv()
    total = jnp.zeros((8, NZ), jnp.float32)
    for k in range(2):
        j = p2[k] * x_in[k]
        jn[4 + mine + k] = j
        for q in range(8):
            total = total + j[8 * q : 8 * q + 8]
    j_to = [(sides[0], 0), (cross_sides[0], 0), (sides[1], 8), (cross_sides[1], 8), (chip, 4)]
    j_c = [
        send(jn.at[pl.ds(4 + mine, 2)], jn.at[pl.ds(at + mine, 2)], j_s.at[i], j_r.at[i], to)
        for i, (to, at) in enumerate(j_to)
    ]
    for c in j_c:
        c.start()
    g_c = [
        send(gc.at[pl.ds(4, 4)], gc.at[pl.ds(8 * i, 4)], g_s.at[i], g_r.at[i], sides[i]) for i in range(2)
    ]
    for c in g_c:
        c.start()
    zs[0] = total
    z_c = [send(zs.at[0], zs.at[k + 1], z_s.at[k], z_r.at[k], z_peer[k]) for k in range(7)]
    for c in z_c:
        c.start()

    count_a = jnp.float32(0.0)
    for a in range(4):
        count_a = count_a + jnp.where(labels[a] == 0, 1.0, 0.0)

    def add(t, p, v):
        for b in range(4):
            acc[b, t, p] = acc[b, t, p] + v[16 * b : 16 * b + 16]

    j_c[4].wait_recv()
    for p in range(4):
        j = 0.25 * jn[4 + p]
        for b in range(4):
            acc[b, 0, p] = count_a * j[16 * b : 16 * b + 16]
            acc[b, 1, p] = (4.0 - count_a) * j[16 * b : 16 * b + 16]

    for a in range(4):
        for i in range(2):
            end_copy(a, i).wait_recv()
    for c in j_c[:4]:
        c.wait_recv()

    def backward(a, _):
        lab = labels[a]
        is_a = lab == 0

        def middle(p, v):
            v = 0.5 * f1s[a, p - 2] * v
            add(0, p - 2, jnp.where(is_a, v, 0.0))
            add(1, p - 2, jnp.where(is_a, 0.0, v))

        contour(
            lambda p: jn[p + 2] * rb[a, p], lambda p: hf[lab, p], lambda p: ff[lab, p], 2, 8, u, w, u2, middle
        )
        return 0

    lax.fori_loop(0, 4, backward, 0)
    for c in z_c:
        c.wait_recv()
    s = zs[0]
    for k in range(1, 8):
        s = s + zs[k]
    ys[0] = s
    pl.semaphore_wait(near_y, 2)
    y_c = [send(ys.at[0], ys.at[k + 1], y_s.at[k], y_r.at[k], y_peer[k]) for k in range(3)]
    for c in y_c:
        c.start()
    for c in g_c:
        c.wait_recv()

    def keep_back(p, v):
        step[p] = v

    contour(
        lambda p: jn[p] * gc[p], lambda p: hf[core, p], lambda p: ff[core, p], 0, 12, u, w, u2, keep_back
    )

    def last(p, v):
        add(core, p - 2, 0.25 * v)

    contour(lambda p: step[p + 2], lambda p: hf[core, p], lambda p: ff[core, p], 2, 8, u, w, u2, last)

    owners = [across, cross, chip]
    d_c = [send(acc.at[to[0]], d_in.at[k], d_s.at[k], d_r.at[k], to) for k, to in enumerate(owners)]
    for c in d_c:
        c.start()
    for c in y_c:
        c.wait_recv()
    xs[0] = (ys[0] + ys[1]) + (ys[2] + ys[3])
    x_c = [send(xs.at[0], xs.at[k + 1], x_s.at[k], x_r.at[k], x_peer[k]) for k in range(3)]
    for c in x_c:
        c.start()
    for c in x_c:
        c.wait_recv()
    s = (xs[0] + xs[1]) + (xs[2] + xs[3])
    s = jnp.sum(jnp.sum(s, axis=0, keepdims=True), axis=1, keepdims=True)
    cells = float(NX * NY * NZ)
    scale = jnp.broadcast_to(1.0 / (ARMS * (s / cells)), (16, NZ))
    rows = pl.ds(pl.multiple_of(16 * me_a, 16), 16)
    for c in d_c:
        c.wait_recv()
    for p in range(4):
        d = [
            scale * ((acc[me_a, t, p] + d_in[2, t, p]) + (d_in[0, t, p] + d_in[1, t, p])) for t in range(2)
        ]
        f = [fld[t, 4 + p, rows] for t in range(2)]
        pressure = 0.5 * (f[0] + f[1] - chi_value)
        for t in range(2):
            density[t, p] = d[t]
            new_fields[t, p] = f[t] + mixing * (chi_value * d[1 - t] + pressure - f[t])
    for a in range(4):
        for i in range(2):
            start_copy(a, i).wait_send()
            end_copy(a, i).wait_send()
    for c in fld_c + fc_c + [pc, gi, px] + g_c + j_c + z_c + y_c + x_c + d_c:
        c.wait_send()


def local(fields, starts, labels):
    vmem = lambda *shape: pltpu.VMEM(shape, jnp.float32)
    dma = lambda *shape: pltpu.SemaphoreType.DMA(shape)
    plane = (NY, NZ)
    return pl.pallas_call(
        kernel,
        out_shape=(jax.ShapeDtypeStruct((2, 4, 16, NZ), jnp.float32),) * 2,
        in_specs=[
            pl.BlockSpec(memory_space=pltpu.HBM),
            pl.BlockSpec(memory_space=pltpu.HBM),
            pl.BlockSpec(memory_space=pltpu.HBM),
        ],
        out_specs=(pl.BlockSpec(memory_space=pltpu.VMEM), pl.BlockSpec(memory_space=pltpu.VMEM)),
        scratch_shapes=[
            pltpu.SMEM((4,), jnp.int32), vmem(2, 12, *plane), vmem(4, 12, *plane), vmem(2, 12, *plane), vmem(2, 12, *plane),
            vmem(12, *plane), vmem(12, *plane), vmem(12, *plane), vmem(12, *plane),
            vmem(4, 4, *plane), vmem(4, 8, *plane), vmem(2, 4, *plane), vmem(4, *plane), vmem(12, *plane),
            vmem(4, *plane), vmem(2, *plane), vmem(2, *plane), vmem(2, *plane), vmem(12, *plane),
            vmem(4, 2, 4, 16, NZ), vmem(3, 2, 4, 16, NZ),
            vmem(8, 8, NZ), vmem(4, 8, NZ), vmem(4, 8, NZ),
            dma(6), dma(2), dma(2), dma(2), dma(2), dma(4, 2), dma(4, 2), dma(4, 2), dma(4, 2),
            pltpu.SemaphoreType.DMA, pltpu.SemaphoreType.DMA, dma(2), dma(2),
            pltpu.SemaphoreType.DMA, pltpu.SemaphoreType.DMA, pltpu.SemaphoreType.DMA, pltpu.SemaphoreType.DMA,
            dma(5), dma(5), dma(3), dma(3), dma(7), dma(7), dma(3), dma(3), dma(3), dma(3),
            pltpu.SemaphoreType.REGULAR, pltpu.SemaphoreType.REGULAR, pltpu.SemaphoreType.REGULAR,
        ],
        compiler_params=pltpu.CompilerParams(collective_id=0, has_side_effects=True, vmem_limit_bytes=56300000),
    )(fields, starts, labels)


def solution(mesh):
    in_specs = (P(None, "space", None, None), P("arm", "space", None, None), P("arm"))
    out_specs = (P(None, "space", "arm", None), P(None, "space", "arm", None))
    return jax.shard_map(local, mesh=mesh, in_specs=in_specs, out_specs=out_specs, check_vma=False)
```

```python
import jax
import jax.numpy as jnp
from jax import lax
from jax.experimental import pallas as pl
from jax.experimental.pallas import tpu as pltpu
from jax.sharding import PartitionSpec as P

coupling_full = 0.15
contour_step = 0.05
chi_value = 2.0
mixing = 0.5
ARMS, NX, NY, NZ = 16, 256, 64, 128
MESH = pl.DeviceIdType.MESH


def stencil(ref, p, c):
    m = ref[p]
    s = ref[p - 1] + ref[p + 1]
    s = s + (pltpu.roll(m, 1, 0) + pltpu.roll(m, NY - 1, 0))
    s = s + (pltpu.roll(m, 1, 1) + pltpu.roll(m, NZ - 1, 1))
    return (1.0 - 6.0 * c) * m + c * s


def contour(value, hf, ff, base, count, u, w, u2, emit):
    for p in range(count):
        v = value(p)
        u[p] = hf(base + p) * v
        w[p] = ff(base + p) * v
    for p in range(1, count - 1):
        u2[p] = ff(base + p) * stencil(u, p, coupling_full / 2)
    for p in range(2, count - 2):
        h = hf(base + p) * stencil(u2, p, coupling_full / 2)
        f = ff(base + p) * stencil(w, p, coupling_full)
        emit(p, (4.0 / 3.0) * h - (1.0 / 3.0) * f)


def kernel(
    fields, starts, labels_hbm, density, new_fields,
    labels, fld, st, hf, ff, u, w, u2, step, f1s, rb, gs, g_in, gh, bo, b0, pr, chip_in, p2, x_in, jn, acc, d_in, zs, ys, xs,
    local_sem, fld_s, fld_r, fc_s, fc_r, st_s, st_r, rb_s, rb_r, gi_s, gi_r, gh_s, gh_r, bo_s, bo_r, pc_s, pc_r, px_s, px_r,
    j_s, j_r, d_s, d_r, z_s, z_r, y_s, y_r, x_s, x_r, near_z, far_z, near_y,
):
    me_a, me_s = lax.axis_index("arm"), lax.axis_index("space")
    up, dn = lax.rem(me_s + 1, 64), lax.rem(me_s + 63, 64)
    core, high = lax.rem(me_a, 2), me_a // 2
    arm_c = high * 2 + 1 - core
    chip = (arm_c, me_s)
    across = ((1 - high) * 2 + core, me_s)
    cross = ((1 - high) * 2 + 1 - core, me_s)
    z = lax.rem(me_s, 8)
    row = me_s // 8
    y, x_lo = row // 2, lax.rem(row, 2)
    z_peer = [(me_a, me_s - z + lax.rem(z + k, 8)) for k in range(1, 8)]
    y_peer = [(me_a, me_s + (lax.rem(y + k, 4) - y) * 16) for k in range(1, 4)]
    x_s_id = me_s + 8 - 16 * x_lo
    x_peer = [(me_a, x_s_id), (arm_c, me_s), (arm_c, x_s_id)]
    sides = [(me_a, up), (me_a, dn)]
    cross_sides = [(arm_c, up), (arm_c, dn)]

    def send(src, dst, ss, rs, to):
        return pltpu.make_async_remote_copy(src, dst, ss, rs, device_id=to, device_id_type=MESH)

    def signal(sem, to):
        pl.semaphore_signal(sem, inc=1, device_id=to, device_id_type=MESH)

    own_l = pltpu.make_async_copy(labels_hbm, labels, local_sem.at[5])
    own_l.start()
    own_f = pltpu.make_async_copy(fields, fld.at[:, pl.ds(4, 4)], local_sem.at[4])
    own_f.start()
    own = [pltpu.make_async_copy(starts.at[a], st.at[a, pl.ds(4, 4)], local_sem.at[a]) for a in range(4)]
    for c in own:
        c.start()

    barrier = pltpu.get_barrier_semaphore()
    near = [z_peer[0], z_peer[6]]
    peers = sides + cross_sides + [chip, across, cross] + near + [y_peer[0], y_peer[2], x_peer[0], x_peer[2]]
    for to in peers:
        signal(barrier, to)
    pl.semaphore_wait(barrier, len(peers))

    own_l.wait()
    own_f.wait()
    fld_c = [
        send(fld.at[core, pl.ds(4, 4)], fld.at[core, pl.ds(8 * i, 4)], fld_s.at[i], fld_r.at[i], sides[i])
        for i in range(2)
    ]
    for c in fld_c:
        c.start()

    def start_copy(a, i):
        return send(st.at[a, pl.ds(4, 4)], st.at[a, pl.ds(8 * i, 4)], st_s.at[a, i], st_r.at[a, i], sides[i])

    def end_copy(a, i):
        return send(
            rb.at[a, pl.ds(4 - 2 * i, 2)], rb.at[a, pl.ds(6 * i, 2)], rb_s.at[a, i], rb_r.at[a, i], sides[i]
        )

    for a in range(4):
        own[a].wait()
        for i in range(2):
            start_copy(a, i).start()
    for to in near:
        signal(near_z, to)
    for k in (0, 2):
        signal(near_y, y_peer[k])
    pr[...] = jnp.ones_like(pr)
    gs[...] = jnp.zeros_like(gs)
    fc_c = [
        send(fld.at[core, pl.ds(8 * i, 4)], fld.at[core, pl.ds(8 * i, 4)], fc_s.at[i], fc_r.at[i], chip)
        for i in range(2)
    ]
    for i in range(2):
        fld_c[i].wait_recv()
        fc_c[i].start()

    pl.semaphore_wait(near_z, 2)
    for k in (1, 5):
        signal(far_z, z_peer[k])
    for c in fc_c:
        c.wait_recv()

    def factor(p, _):
        for t in range(2):
            h = jnp.exp(fld[t, p] * (-contour_step / 4))
            hf[t, p] = h
            ff[t, p] = h * h
        return 0

    lax.fori_loop(0, 12, factor, 0)

    def forward(a, _):
        lab = labels[a]
        is_a = lab == 0
        for i in range(2):
            start_copy(a, i).wait_recv()

        def keep_one(p, v):
            step[p] = v

        contour(lambda p: st[a, p], lambda p: hf[lab, p], lambda p: ff[lab, p], 0, 12, u, w, u2, keep_one)

        def keep_two(p, v):
            own_p = p - 2
            f1s[a, own_p] = step[p + 2]
            r = 1.0 / v
            rb[a, p] = r
            pr[own_p] = pr[own_p] * v
            gs[0, p] = gs[0, p] + jnp.where(is_a, r, 0.0)
            gs[1, p] = gs[1, p] + jnp.where(is_a, 0.0, r)

        contour(
            lambda p: step[p + 2], lambda p: hf[lab, p], lambda p: ff[lab, p], 2, 8, u, w, u2, keep_two
        )
        for i in range(2):
            end_copy(a, i).start()
        return 0

    lax.fori_loop(0, 4, forward, 0)

    mine = 2 * core
    pc = send(pr.at[pl.ds(2 - mine, 2)], chip_in, pc_s, pc_r, chip)
    pc.start()
    gi = send(gs.at[:, pl.ds(4 - mine, 2)], g_in, gi_s, gi_r, chip)
    gi.start()
    pc.wait_recv()
    for k in range(2):
        p2[k] = pr[mine + k] * chip_in[k]
    px = send(p2, x_in, px_s, px_r, across)
    px.start()
    pl.semaphore_wait(far_z, 2)
    px.wait_recv()
    total = jnp.zeros((8, NZ), jnp.float32)
    for k in range(2):
        j = p2[k] * x_in[k]
        jn[4 + mine + k] = j
        for q in range(8):
            total = total + j[8 * q : 8 * q + 8]

    near_side = core * up + (1 - core) * dn
    far_side = core * dn + (1 - core) * up
    half = pl.ds(4 + mine, 2)
    near_at = pl.ds(8 - 6 * core, 2)
    j_c = [
        send(jn.at[half], jn.at[near_at], j_s.at[0], j_r.at[0], (me_a, near_side)),
        send(jn.at[half], jn.at[near_at], j_s.at[1], j_r.at[1], (arm_c, near_side)),
        send(jn.at[half], jn.at[half], j_s.at[2], j_r.at[2], chip),
    ]
    for c in j_c:
        c.start()
    zs[0] = total
    z_c = [send(zs.at[0], zs.at[k + 1], z_s.at[k], z_r.at[k], z_peer[k]) for k in range(7)]
    for c in z_c:
        c.start()

    gi.wait_recv()
    for k in range(2):
        j = jn[4 + mine + k]
        for t in range(2):
            bo[t, k] = j * (gs[t, 2 + mine + k] + g_in[t, k])
        b0[4 + mine + k] = bo[core, k]
    far_at = pl.ds(10 * core, 2)
    bo_c = [
        send(bo.at[1 - core], b0.at[half], bo_s.at[2], bo_r.at[2], chip),
        send(bo.at[core], b0.at[far_at], bo_s.at[0], bo_r.at[0], (me_a, far_side)),
        send(bo.at[1 - core], b0.at[far_at], bo_s.at[1], bo_r.at[1], (arm_c, far_side)),
    ]
    bo_c[0].start()

    for a in range(4):
        is_a = labels[a] == 0
        for i in range(2):
            end_copy(a, i).wait_recv()
        for p in (0, 1, 6, 7):
            r = rb[a, p]
            gs[0, p] = gs[0, p] + jnp.where(is_a, r, 0.0)
            gs[1, p] = gs[1, p] + jnp.where(is_a, 0.0, r)
    gh_c = [
        send(gs.at[1 - core, pl.ds(6 * i, 2)], gh.at[i], gh_s.at[i], gh_r.at[i], chip) for i in range(2)
    ]
    for c in gh_c:
        c.start()
    bo_c[1].start()
    bo_c[2].start()

    count_a = jnp.float32(0.0)
    for a in range(4):
        count_a = count_a + jnp.where(labels[a] == 0, 1.0, 0.0)

    def add(t, p, v):
        for b in range(4):
            acc[b, t, p] = acc[b, t, p] + v[16 * b : 16 * b + 16]

    j_c[2].wait_recv()
    for p in range(4):
        j = 0.25 * jn[4 + p]
        for b in range(4):
            acc[b, 0, p] = count_a * j[16 * b : 16 * b + 16]
            acc[b, 1, p] = (4.0 - count_a) * j[16 * b : 16 * b + 16]

    for c in j_c[:2]:
        c.wait_recv()

    def backward(a, _):
        lab = labels[a]
        is_a = lab == 0

        def middle(p, v):
            v = 0.5 * f1s[a, p - 2] * v
            add(0, p - 2, jnp.where(is_a, v, 0.0))
            add(1, p - 2, jnp.where(is_a, 0.0, v))

        contour(
            lambda p: jn[p + 2] * rb[a, p], lambda p: hf[lab, p], lambda p: ff[lab, p], 2, 8, u, w, u2, middle
        )
        return 0

    lax.fori_loop(0, 4, backward, 0)
    owners = [across, cross, chip]

    def owner_copy(k, late):
        t = core if late else 1 - core
        return send(acc.at[owners[k][0], t], d_in.at[k, t], d_s.at[k, late], d_r.at[k, late], owners[k])

    for k in range(3):
        owner_copy(k, 0).start()
    for c in z_c:
        c.wait_recv()
    s = zs[0]
    for k in range(1, 8):
        s = s + zs[k]
    ys[0] = s
    pl.semaphore_wait(near_y, 2)
    y_c = [send(ys.at[0], ys.at[k + 1], y_s.at[k], y_r.at[k], y_peer[k]) for k in range(3)]
    for c in y_c:
        c.start()
    for i in range(2):
        gh_c[i].wait_recv()
        for k in range(2):
            b0[2 + 6 * i + k] = jn[2 + 6 * i + k] * (gs[core, 6 * i + k] + gh[i, k])
    for c in bo_c:
        c.wait_recv()

    def keep_back(p, v):
        step[p] = v

    contour(
        lambda p: b0[p], lambda p: hf[core, p], lambda p: ff[core, p], 0, 12, u, w, u2, keep_back
    )

    def last(p, v):
        add(core, p - 2, 0.25 * v)

    contour(lambda p: step[p + 2], lambda p: hf[core, p], lambda p: ff[core, p], 2, 8, u, w, u2, last)

    for k in range(3):
        owner_copy(k, 1).start()
    for c in y_c:
        c.wait_recv()
    xs[0] = (ys[0] + ys[1]) + (ys[2] + ys[3])
    x_c = [send(xs.at[0], xs.at[k + 1], x_s.at[k], x_r.at[k], x_peer[k]) for k in range(3)]
    for c in x_c:
        c.start()
    for c in x_c:
        c.wait_recv()
    s = (xs[0] + xs[1]) + (xs[2] + xs[3])
    s = jnp.sum(jnp.sum(s, axis=0, keepdims=True), axis=1, keepdims=True)
    cells = float(NX * NY * NZ)
    scale = jnp.broadcast_to(1.0 / (ARMS * (s / cells)), (16, NZ))
    rows = pl.ds(pl.multiple_of(16 * me_a, 16), 16)
    for k in range(3):
        for late in range(2):
            owner_copy(k, late).wait_recv()
    for p in range(4):
        d = [
            scale * ((acc[me_a, t, p] + d_in[2, t, p]) + (d_in[0, t, p] + d_in[1, t, p])) for t in range(2)
        ]
        f = [fld[t, 4 + p, rows] for t in range(2)]
        pressure = 0.5 * (f[0] + f[1] - chi_value)
        for t in range(2):
            density[t, p] = d[t]
            new_fields[t, p] = f[t] + mixing * (chi_value * d[1 - t] + pressure - f[t])
    for a in range(4):
        for i in range(2):
            start_copy(a, i).wait_send()
            end_copy(a, i).wait_send()
    for k in range(3):
        for late in range(2):
            owner_copy(k, late).wait_send()
    for c in fld_c + fc_c + [pc, gi, px] + gh_c + bo_c + j_c + z_c + y_c + x_c:
        c.wait_send()


def local(fields, starts, labels):
    vmem = lambda *shape: pltpu.VMEM(shape, jnp.float32)
    dma = lambda *shape: pltpu.SemaphoreType.DMA(shape)
    plane = (NY, NZ)
    return pl.pallas_call(
        kernel,
        out_shape=(jax.ShapeDtypeStruct((2, 4, 16, NZ), jnp.float32),) * 2,
        in_specs=[
            pl.BlockSpec(memory_space=pltpu.HBM),
            pl.BlockSpec(memory_space=pltpu.HBM),
            pl.BlockSpec(memory_space=pltpu.HBM),
        ],
        out_specs=(pl.BlockSpec(memory_space=pltpu.VMEM), pl.BlockSpec(memory_space=pltpu.VMEM)),
        scratch_shapes=[
            pltpu.SMEM((4,), jnp.int32), vmem(2, 12, *plane), vmem(4, 12, *plane), vmem(2, 12, *plane), vmem(2, 12, *plane),
            vmem(12, *plane), vmem(12, *plane), vmem(12, *plane), vmem(12, *plane),
            vmem(4, 4, *plane), vmem(4, 8, *plane), vmem(2, 8, *plane), vmem(2, 2, *plane), vmem(2, 2, *plane), vmem(2, 2, *plane), vmem(12, *plane),
            vmem(4, *plane), vmem(2, *plane), vmem(2, *plane), vmem(2, *plane), vmem(12, *plane),
            vmem(4, 2, 4, 16, NZ), vmem(3, 2, 4, 16, NZ),
            vmem(8, 8, NZ), vmem(4, 8, NZ), vmem(4, 8, NZ),
            dma(6), dma(2), dma(2), dma(2), dma(2), dma(4, 2), dma(4, 2), dma(4, 2), dma(4, 2),
            pltpu.SemaphoreType.DMA, pltpu.SemaphoreType.DMA, dma(2), dma(2), dma(3), dma(3),
            pltpu.SemaphoreType.DMA, pltpu.SemaphoreType.DMA, pltpu.SemaphoreType.DMA, pltpu.SemaphoreType.DMA,
            dma(3), dma(3), dma(3, 2), dma(3, 2), dma(7), dma(7), dma(3), dma(3), dma(3), dma(3),
            pltpu.SemaphoreType.REGULAR, pltpu.SemaphoreType.REGULAR, pltpu.SemaphoreType.REGULAR,
        ],
        compiler_params=pltpu.CompilerParams(collective_id=0, has_side_effects=True, vmem_limit_bytes=56300000),
    )(fields, starts, labels)


def solution(mesh):
    in_specs = (P(None, "space", None, None), P("arm", "space", None, None), P("arm"))
    out_specs = (P(None, "space", "arm", None), P(None, "space", "arm", None))
    return jax.shard_map(local, mesh=mesh, in_specs=in_specs, out_specs=out_specs, check_vma=False)
```

```python
import jax
import jax.numpy as jnp
from jax import lax
from jax.experimental import pallas as pl
from jax.experimental.pallas import tpu as pltpu
from jax.sharding import PartitionSpec as P

coupling_full = 0.15
contour_step = 0.05
chi_value = 2.0
mixing = 0.5
ARMS, NX, NY, NZ = 16, 256, 64, 128
MESH = pl.DeviceIdType.MESH


def stencil(ref, p, c):
    m = ref[p]
    s = ref[p - 1] + ref[p + 1]
    s = s + (pltpu.roll(m, 1, 0) + pltpu.roll(m, NY - 1, 0))
    s = s + (pltpu.roll(m, 1, 1) + pltpu.roll(m, NZ - 1, 1))
    return (1.0 / c - 6.0) * m + s


def contour(value, fac, base, count, u, w, u2, emit):
    for p in range(count):
        v = value(p)
        u[p] = fac(0, base + p) * v
        w[p] = fac(1, base + p) * v
    for p in range(1, count - 1):
        u2[p] = fac(2, base + p) * stencil(u, p, coupling_full / 2)
    for p in range(2, count - 2):
        h = fac(3, base + p) * stencil(u2, p, coupling_full / 2)
        f = fac(4, base + p) * stencil(w, p, coupling_full)
        emit(p, h - f)


def kernel(
    fields, starts, labels_hbm, out,
    labels, fld, st, fa, u, w, u2, step, f1s, rb, gs, g_in, gh, bo, b0, pr, chip_in, p2, x_in, jn, acc, d_in, zs, ys,
    local_sem, fld_s, fld_r, fc_s, fc_r, st_s, st_r, rb_s, rb_r, gi_s, gi_r, gh_s, gh_r, bo_s, bo_r, pc_s, pc_r, px_s, px_r,
    j_s, j_r, d_s, d_r, z_s, z_r, y_s, y_r, near_z, far_z, near_y, near_x,
):
    me_a, me_s = lax.axis_index("arm"), lax.axis_index("space")
    up, dn = lax.rem(me_s + 1, 64), lax.rem(me_s + 63, 64)
    core, high = lax.rem(me_a, 2), me_a // 2
    arm_c = high * 2 + 1 - core
    chip = (arm_c, me_s)
    across = ((1 - high) * 2 + core, me_s)
    cross = ((1 - high) * 2 + 1 - core, me_s)
    z = lax.rem(me_s, 8)
    row = me_s // 8
    y, x_lo = row // 2, lax.rem(row, 2)
    z_peer = [(me_a, me_s - z + lax.rem(z + k, 8)) for k in range(1, 8)]
    y_peer = [(me_a, me_s + (lax.rem(y + k, 4) - y) * 16) for k in range(1, 4)]
    x_s_id = me_s + 8 - 16 * x_lo
    x_peer = [(me_a, x_s_id), (arm_c, me_s), (arm_c, x_s_id)]
    wide_peer = y_peer + [
        (to[0], to[1] + (lax.rem(y + k, 4) - y) * 16) for to in x_peer for k in range(4)
    ]
    sides = [(me_a, up), (me_a, dn)]
    cross_sides = [(arm_c, up), (arm_c, dn)]

    def send(src, dst, ss, rs, to):
        return pltpu.make_async_remote_copy(src, dst, ss, rs, device_id=to, device_id_type=MESH)

    def signal(sem, to):
        pl.semaphore_signal(sem, inc=1, device_id=to, device_id_type=MESH)

    own_l = pltpu.make_async_copy(labels_hbm, labels, local_sem.at[5])
    own_l.start()
    own_f = pltpu.make_async_copy(fields, fld.at[:, pl.ds(4, 4)], local_sem.at[4])
    own_f.start()
    own = [pltpu.make_async_copy(starts.at[a], st.at[a, pl.ds(4, 4)], local_sem.at[a]) for a in range(4)]
    for c in own:
        c.start()

    barrier = pltpu.get_barrier_semaphore()
    near = [z_peer[0], z_peer[6]]
    peers = sides + cross_sides + [chip, across, cross] + near + [y_peer[0], y_peer[2], x_peer[0], x_peer[2]]
    for to in peers:
        signal(barrier, to)
    pl.semaphore_wait(barrier, len(peers))

    own_l.wait()
    own_f.wait()
    fld_c = [
        send(fld.at[core, pl.ds(4, 4)], fld.at[core, pl.ds(8 * i, 4)], fld_s.at[i], fld_r.at[i], sides[i])
        for i in range(2)
    ]
    for c in fld_c:
        c.start()

    def start_copy(a, i):
        return send(st.at[a, pl.ds(4, 4)], st.at[a, pl.ds(8 * i, 4)], st_s.at[a, i], st_r.at[a, i], sides[i])

    def end_copy(a, i):
        return send(
            rb.at[a, pl.ds(4 - 2 * i, 2)], rb.at[a, pl.ds(6 * i, 2)], rb_s.at[a, i], rb_r.at[a, i], sides[i]
        )

    for a in range(4):
        own[a].wait()
    for a in range(2):
        for i in range(2):
            start_copy(a, i).start()
    for to in near:
        signal(near_z, to)
    for k in (0, 2):
        signal(near_y, y_peer[k])
    pr[...] = jnp.ones_like(pr)
    gs[...] = jnp.zeros_like(gs)
    fc_c = [
        send(fld.at[core, pl.ds(8 * i, 4)], fld.at[core, pl.ds(8 * i, 4)], fc_s.at[i], fc_r.at[i], chip)
        for i in range(2)
    ]
    for i in range(2):
        fld_c[i].wait_recv()
        fc_c[i].start()
    for a in range(2, 4):
        for i in range(2):
            start_copy(a, i).start()

    pl.semaphore_wait(near_z, 2)
    for k in (1, 5):
        signal(far_z, z_peer[k])
    pl.semaphore_wait(near_y, 2)
    for to in x_peer:
        signal(near_x, to)
    for c in fc_c:
        c.wait_recv()

    def factor(p, _):
        for t in range(2):
            h = jnp.exp(fld[t, p] * (-contour_step / 4))
            f = h * h
            fa[t, 0, p] = h
            fa[t, 1, p] = f
            fa[t, 2, p] = (coupling_full / 2) * f
            fa[t, 3, p] = (4.0 / 3.0 * coupling_full / 2) * h
            fa[t, 4, p] = (1.0 / 3.0 * coupling_full) * f
        return 0

    lax.fori_loop(0, 12, factor, 0)

    def forward(a, _):
        lab = labels[a]
        is_a = lab == 0
        for i in range(2):
            start_copy(a, i).wait_recv()

        def keep_one(p, v):
            step[p] = v

        contour(lambda p: st[a, p], lambda i, p: fa[lab, i, p], 0, 12, u, w, u2, keep_one)

        def keep_two(p, v):
            own_p = p - 2
            f1s[a, own_p] = step[p + 2]
            r = 1.0 / v
            rb[a, p] = r
            pr[own_p] = pr[own_p] * v
            gs[0, p] = gs[0, p] + jnp.where(is_a, r, 0.0)
            gs[1, p] = gs[1, p] + jnp.where(is_a, 0.0, r)

        contour(
            lambda p: step[p + 2], lambda i, p: fa[lab, i, p], 2, 8, u, w, u2, keep_two
        )
        @pl.when(a < 3)
        def _():
            for i in range(2):
                end_copy(a, i).start()

        return 0

    lax.fori_loop(0, 4, forward, 0)

    mine = 2 * core
    pc = send(pr.at[pl.ds(2 - mine, 2)], chip_in, pc_s, pc_r, chip)
    pc.start()
    for i in range(2):
        end_copy(3, i).start()
    gi = send(gs.at[:, pl.ds(4 - mine, 2)], g_in, gi_s, gi_r, chip)
    pc.wait_recv()
    for k in range(2):
        p2[k] = pr[mine + k] * chip_in[k]
    px = send(p2, x_in, px_s, px_r, across)
    px.start()
    gi.start()
    pl.semaphore_wait(far_z, 2)
    px.wait_recv()
    total = jnp.zeros((8, NZ), jnp.float32)
    for k in range(2):
        j = p2[k] * x_in[k]
        jn[4 + mine + k] = j
        for q in range(8):
            total = total + j[8 * q : 8 * q + 8]

    near_side = core * up + (1 - core) * dn
    far_side = core * dn + (1 - core) * up
    half = pl.ds(4 + mine, 2)
    near_at = pl.ds(8 - 6 * core, 2)
    j_c = [
        send(jn.at[half], jn.at[near_at], j_s.at[0], j_r.at[0], (me_a, near_side)),
        send(jn.at[half], jn.at[near_at], j_s.at[1], j_r.at[1], (arm_c, near_side)),
        send(jn.at[half], jn.at[half], j_s.at[2], j_r.at[2], chip),
    ]
    for c in j_c:
        c.start()
    zs[0] = total
    z_c = [send(zs.at[0], zs.at[k + 1], z_s.at[k], z_r.at[k], z_peer[k]) for k in range(7)]
    for c in z_c:
        c.start()

    gi.wait_recv()
    for k in range(2):
        j = jn[4 + mine + k]
        for t in range(2):
            bo[t, k] = j * (gs[t, 2 + mine + k] + g_in[t, k])
        b0[4 + mine + k] = bo[core, k]
    far_at = pl.ds(10 * core, 2)
    bo_c = [
        send(bo.at[1 - core], b0.at[half], bo_s.at[2], bo_r.at[2], chip),
        send(bo.at[core], b0.at[far_at], bo_s.at[0], bo_r.at[0], (me_a, far_side)),
        send(bo.at[1 - core], b0.at[far_at], bo_s.at[1], bo_r.at[1], (arm_c, far_side)),
    ]
    bo_c[0].start()

    for a in range(4):
        is_a = labels[a] == 0
        for i in range(2):
            end_copy(a, i).wait_recv()
        for p in (0, 1, 6, 7):
            r = rb[a, p]
            gs[0, p] = gs[0, p] + jnp.where(is_a, r, 0.0)
            gs[1, p] = gs[1, p] + jnp.where(is_a, 0.0, r)
    gh_c = [
        send(gs.at[1 - core, pl.ds(6 * i, 2)], gh.at[i], gh_s.at[i], gh_r.at[i], chip) for i in range(2)
    ]
    for c in gh_c:
        c.start()
    bo_c[1].start()
    bo_c[2].start()

    count_a = jnp.float32(0.0)
    for a in range(4):
        count_a = count_a + jnp.where(labels[a] == 0, 1.0, 0.0)

    def add(t, p, v):
        for b in range(4):
            acc[b, t, p] = acc[b, t, p] + v[16 * b : 16 * b + 16]

    j_c[2].wait_recv()
    for p in range(4):
        j = 0.25 * jn[4 + p]
        for b in range(4):
            acc[b, 0, p] = count_a * j[16 * b : 16 * b + 16]
            acc[b, 1, p] = (4.0 - count_a) * j[16 * b : 16 * b + 16]

    for c in j_c[:2]:
        c.wait_recv()

    for c in z_c:
        c.wait_recv()
    s = zs[0]
    for k in range(1, 8):
        s = s + zs[k]
    ys[0] = s
    pl.semaphore_wait(near_x, 3)
    y_c = [send(ys.at[0], ys.at[k + 1], y_s.at[k], y_r.at[k], wide_peer[k]) for k in range(15)]
    for c in y_c:
        c.start()
    def backward(a, _):
        lab = labels[a]
        is_a = lab == 0

        def middle(p, v):
            v = 0.5 * f1s[a, p - 2] * v
            add(0, p - 2, jnp.where(is_a, v, 0.0))
            add(1, p - 2, jnp.where(is_a, 0.0, v))

        contour(
            lambda p: jn[p + 2] * rb[a, p], lambda i, p: fa[lab, i, p], 2, 8, u, w, u2, middle
        )
        return 0

    lax.fori_loop(0, 4, backward, 0)
    owners = [across, cross, chip]

    def owner_copy(k, late):
        t = core if late else 1 - core
        return send(acc.at[owners[k][0], t], d_in.at[k, t], d_s.at[k, late], d_r.at[k, late], owners[k])

    for k in range(3):
        owner_copy(k, 0).start()
    for i in range(2):
        gh_c[i].wait_recv()
        for k in range(2):
            b0[2 + 6 * i + k] = jn[2 + 6 * i + k] * (gs[core, 6 * i + k] + gh[i, k])
    for c in bo_c:
        c.wait_recv()

    def keep_back(p, v):
        step[p] = v

    contour(
        lambda p: b0[p], lambda i, p: fa[core, i, p], 0, 12, u, w, u2, keep_back
    )

    def last(p, v):
        add(core, p - 2, 0.25 * v)

    contour(lambda p: step[p + 2], lambda i, p: fa[core, i, p], 2, 8, u, w, u2, last)

    for k in range(3):
        owner_copy(k, 1).start()
    for c in y_c:
        c.wait_recv()
    s = ys[0]
    for k in range(1, 16):
        s = s + ys[k]
    s = jnp.sum(jnp.sum(s, axis=0, keepdims=True), axis=1, keepdims=True)
    cells = float(NX * NY * NZ)
    scale = jnp.broadcast_to(1.0 / (ARMS * (s / cells)), (16, NZ))
    rows = pl.ds(pl.multiple_of(16 * me_a, 16), 16)
    for k in range(3):
        for late in range(2):
            owner_copy(k, late).wait_recv()
    for p in range(4):
        d = [
            scale * ((acc[me_a, t, p] + d_in[2, t, p]) + (d_in[0, t, p] + d_in[1, t, p])) for t in range(2)
        ]
        f = [fld[t, 4 + p, rows] for t in range(2)]
        pressure = 0.5 * (f[0] + f[1] - chi_value)
        for t in range(2):
            out[0, t, p] = d[t]
            out[1, t, p] = f[t] + mixing * (chi_value * d[1 - t] + pressure - f[t])
    for a in range(4):
        for i in range(2):
            start_copy(a, i).wait_send()
            end_copy(a, i).wait_send()
    for k in range(3):
        for late in range(2):
            owner_copy(k, late).wait_send()
    for c in fld_c + fc_c + [pc, gi, px] + gh_c + bo_c + j_c + z_c + y_c:
        c.wait_send()


def local(fields, starts, labels):
    vmem = lambda *shape: pltpu.VMEM(shape, jnp.float32)
    dma = lambda *shape: pltpu.SemaphoreType.DMA(shape)
    plane = (NY, NZ)
    out = pl.pallas_call(
        kernel,
        out_shape=jax.ShapeDtypeStruct((2, 2, 4, 16, NZ), jnp.float32),
        in_specs=[
            pl.BlockSpec(memory_space=pltpu.HBM),
            pl.BlockSpec(memory_space=pltpu.HBM),
            pl.BlockSpec(memory_space=pltpu.HBM),
        ],
        out_specs=pl.BlockSpec(memory_space=pltpu.VMEM),
        scratch_shapes=[
            pltpu.SMEM((4,), jnp.int32), vmem(2, 12, *plane), vmem(4, 12, *plane), vmem(2, 5, 12, *plane),
            vmem(12, *plane), vmem(12, *plane), vmem(12, *plane), vmem(12, *plane),
            vmem(4, 4, *plane), vmem(4, 8, *plane), vmem(2, 8, *plane), vmem(2, 2, *plane), vmem(2, 2, *plane), vmem(2, 2, *plane), vmem(12, *plane),
            vmem(4, *plane), vmem(2, *plane), vmem(2, *plane), vmem(2, *plane), vmem(12, *plane),
            vmem(4, 2, 4, 16, NZ), vmem(3, 2, 4, 16, NZ),
            vmem(8, 8, NZ), vmem(16, 8, NZ),
            dma(6), dma(2), dma(2), dma(2), dma(2), dma(4, 2), dma(4, 2), dma(4, 2), dma(4, 2),
            pltpu.SemaphoreType.DMA, pltpu.SemaphoreType.DMA, dma(2), dma(2), dma(3), dma(3),
            pltpu.SemaphoreType.DMA, pltpu.SemaphoreType.DMA, pltpu.SemaphoreType.DMA, pltpu.SemaphoreType.DMA,
            dma(3), dma(3), dma(3, 2), dma(3, 2), dma(7), dma(7), dma(15), dma(15),
            pltpu.SemaphoreType.REGULAR, pltpu.SemaphoreType.REGULAR, pltpu.SemaphoreType.REGULAR, pltpu.SemaphoreType.REGULAR,
        ],
        compiler_params=pltpu.CompilerParams(collective_id=0, has_side_effects=True, vmem_limit_bytes=56300000),
    )(fields, starts, labels)
    return out[0], out[1]


def solution(mesh):
    in_specs = (P(None, "space", None, None), P("arm", "space", None, None), P("arm"))
    out_specs = (P(None, "space", "arm", None), P(None, "space", "arm", None))
    return jax.shard_map(local, mesh=mesh, in_specs=in_specs, out_specs=out_specs, check_vma=False)
```

```python
import jax
import jax.numpy as jnp
from jax import lax
from jax.experimental import pallas as pl
from jax.experimental.pallas import tpu as pltpu
from jax.sharding import PartitionSpec as P

coupling_full = 0.15
contour_step = 0.05
chi_value = 2.0
mixing = 0.5
ARMS, NX, NY, NZ = 16, 256, 64, 128
MESH = pl.DeviceIdType.MESH


def stencil(ref, p, c):
    m = ref[p]
    s = ref[p - 1] + ref[p + 1]
    s = s + (pltpu.roll(m, 1, 0) + pltpu.roll(m, NY - 1, 0))
    s = s + (pltpu.roll(m, 1, 1) + pltpu.roll(m, NZ - 1, 1))
    return (1.0 / c - 6.0) * m + s


def contour(value, fac, base, count, u, w, u2, emit):
    for p in range(count):
        v = value(p)
        u[p] = fac(0, base + p) * v
        w[p] = fac(1, base + p) * v
    for p in range(1, count - 1):
        u2[p] = fac(2, base + p) * stencil(u, p, coupling_full / 2)
    for p in range(2, count - 2):
        h = fac(3, base + p) * stencil(u2, p, coupling_full / 2)
        f = fac(4, base + p) * stencil(w, p, coupling_full)
        emit(p, h - f)


def kernel(
    fields, starts, labels_hbm, out,
    labels, fld, st, fa, u, w, u2, step, f1s, rb, gs, g_in, gh, bo, b0, pr, chip_in, p2, x_in, jn, acc, d_in, d_out, zs, ys,
    local_sem, fld_s, fld_r, fc_s, fc_r, st_s, st_r, rb_s, rb_r, gi_s, gi_r, gh_s, gh_r, bo_s, bo_r, pc_s, pc_r, px_s, px_r,
    j_s, j_r, d_s, d_r, dx_s, dx_r, z_s, z_r, y_s, y_r, near_z, far_z, near_y, near_x,
):
    me_a, me_s = lax.axis_index("arm"), lax.axis_index("space")
    up, dn = lax.rem(me_s + 1, 64), lax.rem(me_s + 63, 64)
    core, high = lax.rem(me_a, 2), me_a // 2
    arm_c = high * 2 + 1 - core
    chip = (arm_c, me_s)
    across = ((1 - high) * 2 + core, me_s)
    cross = ((1 - high) * 2 + 1 - core, me_s)
    z = lax.rem(me_s, 8)
    row = me_s // 8
    y, x_lo = row // 2, lax.rem(row, 2)
    z_peer = [(me_a, me_s - z + lax.rem(z + k, 8)) for k in range(1, 8)]
    y_peer = [(me_a, me_s + (lax.rem(y + k, 4) - y) * 16) for k in range(1, 4)]
    x_s_id = me_s + 8 - 16 * x_lo
    x_peer = [(me_a, x_s_id), (arm_c, me_s), (arm_c, x_s_id)]
    wide_peer = y_peer + [
        (to[0], to[1] + (lax.rem(y + k, 4) - y) * 16) for to in x_peer for k in range(4)
    ]
    sides = [(me_a, up), (me_a, dn)]
    cross_sides = [(arm_c, up), (arm_c, dn)]

    def send(src, dst, ss, rs, to):
        return pltpu.make_async_remote_copy(src, dst, ss, rs, device_id=to, device_id_type=MESH)

    def signal(sem, to):
        pl.semaphore_signal(sem, inc=1, device_id=to, device_id_type=MESH)

    own_l = pltpu.make_async_copy(labels_hbm, labels, local_sem.at[5])
    own_l.start()
    own_f = pltpu.make_async_copy(fields, fld.at[:, pl.ds(4, 4)], local_sem.at[4])
    own_f.start()
    own = [pltpu.make_async_copy(starts.at[a], st.at[a, pl.ds(4, 4)], local_sem.at[a]) for a in range(4)]
    for c in own:
        c.start()

    barrier = pltpu.get_barrier_semaphore()
    near = [z_peer[0], z_peer[6]]
    peers = sides + cross_sides + [chip, across, cross] + near + [y_peer[0], y_peer[2], x_peer[0], x_peer[2]]
    for to in peers:
        signal(barrier, to)
    pl.semaphore_wait(barrier, len(peers))

    own_l.wait()
    own_f.wait()
    fld_c = [
        send(fld.at[core, pl.ds(4, 4)], fld.at[core, pl.ds(8 * i, 4)], fld_s.at[i], fld_r.at[i], sides[i])
        for i in range(2)
    ]
    for c in fld_c:
        c.start()

    def start_copy(a, i):
        return send(st.at[a, pl.ds(4, 4)], st.at[a, pl.ds(8 * i, 4)], st_s.at[a, i], st_r.at[a, i], sides[i])

    def end_copy(a, i):
        return send(
            rb.at[a, pl.ds(4 - 2 * i, 2)], rb.at[a, pl.ds(6 * i, 2)], rb_s.at[a, i], rb_r.at[a, i], sides[i]
        )

    for a in range(4):
        own[a].wait()
    for a in range(2):
        for i in range(2):
            start_copy(a, i).start()
    for to in near:
        signal(near_z, to)
    for k in (0, 2):
        signal(near_y, y_peer[k])
    pr[...] = jnp.ones_like(pr)
    gs[...] = jnp.zeros_like(gs)
    fc_c = [
        send(fld.at[core, pl.ds(8 * i, 4)], fld.at[core, pl.ds(8 * i, 4)], fc_s.at[i], fc_r.at[i], chip)
        for i in range(2)
    ]
    for i in range(2):
        fld_c[i].wait_recv()
        fc_c[i].start()
    for a in range(2, 4):
        for i in range(2):
            start_copy(a, i).start()

    pl.semaphore_wait(near_z, 2)
    for k in (1, 5):
        signal(far_z, z_peer[k])
    pl.semaphore_wait(near_y, 2)
    for to in x_peer:
        signal(near_x, to)
    for c in fc_c:
        c.wait_recv()

    def factor(p, _):
        for t in range(2):
            h = jnp.exp(fld[t, p] * (-contour_step / 4))
            f = h * h
            fa[t, 0, p] = h
            fa[t, 1, p] = f
            fa[t, 2, p] = (coupling_full / 2) * f
            fa[t, 3, p] = (4.0 / 3.0 * coupling_full / 2) * h
            fa[t, 4, p] = (1.0 / 3.0 * coupling_full) * f
        return 0

    lax.fori_loop(0, 12, factor, 0)

    def forward(a, _):
        lab = labels[a]
        is_a = lab == 0
        for i in range(2):
            start_copy(a, i).wait_recv()

        def keep_one(p, v):
            step[p] = v

        contour(lambda p: st[a, p], lambda i, p: fa[lab, i, p], 0, 12, u, w, u2, keep_one)

        def keep_two(p, v):
            own_p = p - 2
            f1s[a, own_p] = step[p + 2]
            r = 1.0 / v
            rb[a, p] = r
            pr[own_p] = pr[own_p] * v
            gs[0, p] = gs[0, p] + jnp.where(is_a, r, 0.0)
            gs[1, p] = gs[1, p] + jnp.where(is_a, 0.0, r)

        contour(
            lambda p: step[p + 2], lambda i, p: fa[lab, i, p], 2, 8, u, w, u2, keep_two
        )
        @pl.when(a < 3)
        def _():
            for i in range(2):
                end_copy(a, i).start()

        return 0

    lax.fori_loop(0, 4, forward, 0)

    mine = 2 * core
    pc = send(pr.at[pl.ds(2 - mine, 2)], chip_in, pc_s, pc_r, chip)
    pc.start()
    for i in range(2):
        end_copy(3, i).start()
    gi = send(gs.at[:, pl.ds(4 - mine, 2)], g_in, gi_s, gi_r, chip)
    pc.wait_recv()
    for k in range(2):
        p2[k] = pr[mine + k] * chip_in[k]
    px = send(p2, x_in, px_s, px_r, across)
    px.start()
    gi.start()
    pl.semaphore_wait(far_z, 2)
    px.wait_recv()
    total = jnp.zeros((8, NZ), jnp.float32)
    for k in range(2):
        j = p2[k] * x_in[k]
        jn[4 + mine + k] = j
        for q in range(8):
            total = total + j[8 * q : 8 * q + 8]

    near_side = core * up + (1 - core) * dn
    far_side = core * dn + (1 - core) * up
    half = pl.ds(4 + mine, 2)
    near_at = pl.ds(8 - 6 * core, 2)
    j_c = [
        send(jn.at[half], jn.at[near_at], j_s.at[0], j_r.at[0], (me_a, near_side)),
        send(jn.at[half], jn.at[near_at], j_s.at[1], j_r.at[1], (arm_c, near_side)),
        send(jn.at[half], jn.at[half], j_s.at[2], j_r.at[2], chip),
    ]
    for c in j_c:
        c.start()
    zs[0] = total
    z_c = [send(zs.at[0], zs.at[k + 1], z_s.at[k], z_r.at[k], z_peer[k]) for k in range(7)]
    for c in z_c:
        c.start()

    gi.wait_recv()
    for k in range(2):
        j = jn[4 + mine + k]
        for t in range(2):
            bo[t, k] = j * (gs[t, 2 + mine + k] + g_in[t, k])
        b0[4 + mine + k] = bo[core, k]
    far_at = pl.ds(10 * core, 2)
    bo_c = [
        send(bo.at[1 - core], b0.at[half], bo_s.at[2], bo_r.at[2], chip),
        send(bo.at[core], b0.at[far_at], bo_s.at[0], bo_r.at[0], (me_a, far_side)),
        send(bo.at[1 - core], b0.at[far_at], bo_s.at[1], bo_r.at[1], (arm_c, far_side)),
    ]
    bo_c[0].start()

    for a in range(4):
        is_a = labels[a] == 0
        for i in range(2):
            end_copy(a, i).wait_recv()
        for p in (0, 1, 6, 7):
            r = rb[a, p]
            gs[0, p] = gs[0, p] + jnp.where(is_a, r, 0.0)
            gs[1, p] = gs[1, p] + jnp.where(is_a, 0.0, r)
    gh_c = [
        send(gs.at[1 - core, pl.ds(6 * i, 2)], gh.at[i], gh_s.at[i], gh_r.at[i], chip) for i in range(2)
    ]
    for c in gh_c:
        c.start()
    bo_c[1].start()
    bo_c[2].start()

    count_a = jnp.float32(0.0)
    for a in range(4):
        count_a = count_a + jnp.where(labels[a] == 0, 1.0, 0.0)

    def add(t, p, v):
        for b in range(4):
            acc[b, t, p] = acc[b, t, p] + v[16 * b : 16 * b + 16]

    j_c[2].wait_recv()
    for p in range(4):
        j = 0.25 * jn[4 + p]
        for b in range(4):
            acc[b, 0, p] = count_a * j[16 * b : 16 * b + 16]
            acc[b, 1, p] = (4.0 - count_a) * j[16 * b : 16 * b + 16]

    for c in j_c[:2]:
        c.wait_recv()

    for c in z_c:
        c.wait_recv()
    s = zs[0]
    for k in range(1, 8):
        s = s + zs[k]
    ys[0] = s
    pl.semaphore_wait(near_x, 3)
    y_c = [send(ys.at[0], ys.at[k + 1], y_s.at[k], y_r.at[k], wide_peer[k]) for k in range(15)]
    for c in y_c:
        c.start()
    def backward(a, _):
        lab = labels[a]
        is_a = lab == 0

        def middle(p, v):
            v = 0.5 * f1s[a, p - 2] * v
            add(0, p - 2, jnp.where(is_a, v, 0.0))
            add(1, p - 2, jnp.where(is_a, 0.0, v))

        contour(
            lambda p: jn[p + 2] * rb[a, p], lambda i, p: fa[lab, i, p], 2, 8, u, w, u2, middle
        )
        return 0

    lax.fori_loop(0, 4, backward, 0)
    blocks = [cross[0], arm_c]

    def owner_copy(k, late):
        t = core if late else 1 - core
        return send(acc.at[blocks[k], t], d_in.at[k, t], d_s.at[k, late], d_r.at[k, late], chip)

    for k in range(2):
        owner_copy(k, 0).start()
    for i in range(2):
        gh_c[i].wait_recv()
        for k in range(2):
            b0[2 + 6 * i + k] = jn[2 + 6 * i + k] * (gs[core, 6 * i + k] + gh[i, k])
    for c in bo_c:
        c.wait_recv()

    def keep_back(p, v):
        step[p] = v

    contour(
        lambda p: b0[p], lambda i, p: fa[core, i, p], 0, 12, u, w, u2, keep_back
    )

    def last(p, v):
        add(core, p - 2, 0.25 * v)

    contour(lambda p: step[p + 2], lambda i, p: fa[core, i, p], 2, 8, u, w, u2, last)

    for k in range(2):
        owner_copy(k, 1).start()
    for late in range(2):
        owner_copy(0, late).wait_recv()
    for t in range(2):
        for p in range(4):
            d_out[t, p] = acc[across[0], t, p] + d_in[0, t, p]
    d_c = send(d_out, d_in.at[2], dx_s, dx_r, across)
    d_c.start()
    for c in y_c:
        c.wait_recv()
    s = ys[0]
    for k in range(1, 16):
        s = s + ys[k]
    s = jnp.sum(jnp.sum(s, axis=0, keepdims=True), axis=1, keepdims=True)
    cells = float(NX * NY * NZ)
    scale = jnp.broadcast_to(1.0 / (ARMS * (s / cells)), (16, NZ))
    rows = pl.ds(pl.multiple_of(16 * me_a, 16), 16)
    for late in range(2):
        owner_copy(1, late).wait_recv()
    d_c.wait_recv()
    for p in range(4):
        d = [
            scale * ((acc[me_a, t, p] + d_in[1, t, p]) + d_in[2, t, p]) for t in range(2)
        ]
        f = [fld[t, 4 + p, rows] for t in range(2)]
        pressure = 0.5 * (f[0] + f[1] - chi_value)
        for t in range(2):
            out[0, t, p] = d[t]
            out[1, t, p] = f[t] + mixing * (chi_value * d[1 - t] + pressure - f[t])
    for a in range(4):
        for i in range(2):
            start_copy(a, i).wait_send()
            end_copy(a, i).wait_send()
    for k in range(2):
        for late in range(2):
            owner_copy(k, late).wait_send()
    d_c.wait_send()
    for c in fld_c + fc_c + [pc, gi, px] + gh_c + bo_c + j_c + z_c + y_c:
        c.wait_send()


def local(fields, starts, labels):
    vmem = lambda *shape: pltpu.VMEM(shape, jnp.float32)
    dma = lambda *shape: pltpu.SemaphoreType.DMA(shape)
    plane = (NY, NZ)
    out = pl.pallas_call(
        kernel,
        out_shape=jax.ShapeDtypeStruct((2, 2, 4, 16, NZ), jnp.float32),
        in_specs=[
            pl.BlockSpec(memory_space=pltpu.HBM),
            pl.BlockSpec(memory_space=pltpu.HBM),
            pl.BlockSpec(memory_space=pltpu.HBM),
        ],
        out_specs=pl.BlockSpec(memory_space=pltpu.VMEM),
        scratch_shapes=[
            pltpu.SMEM((4,), jnp.int32), vmem(2, 12, *plane), vmem(4, 12, *plane), vmem(2, 5, 12, *plane),
            vmem(12, *plane), vmem(12, *plane), vmem(12, *plane), vmem(12, *plane),
            vmem(4, 4, *plane), vmem(4, 8, *plane), vmem(2, 8, *plane), vmem(2, 2, *plane), vmem(2, 2, *plane), vmem(2, 2, *plane), vmem(12, *plane),
            vmem(4, *plane), vmem(2, *plane), vmem(2, *plane), vmem(2, *plane), vmem(12, *plane),
            vmem(4, 2, 4, 16, NZ), vmem(3, 2, 4, 16, NZ), vmem(2, 4, 16, NZ),
            vmem(8, 8, NZ), vmem(16, 8, NZ),
            dma(6), dma(2), dma(2), dma(2), dma(2), dma(4, 2), dma(4, 2), dma(4, 2), dma(4, 2),
            pltpu.SemaphoreType.DMA, pltpu.SemaphoreType.DMA, dma(2), dma(2), dma(3), dma(3),
            pltpu.SemaphoreType.DMA, pltpu.SemaphoreType.DMA, pltpu.SemaphoreType.DMA, pltpu.SemaphoreType.DMA,
            dma(3), dma(3), dma(2, 2), dma(2, 2), pltpu.SemaphoreType.DMA, pltpu.SemaphoreType.DMA, dma(7), dma(7), dma(15), dma(15),
            pltpu.SemaphoreType.REGULAR, pltpu.SemaphoreType.REGULAR, pltpu.SemaphoreType.REGULAR, pltpu.SemaphoreType.REGULAR,
        ],
        compiler_params=pltpu.CompilerParams(collective_id=0, has_side_effects=True, vmem_limit_bytes=56300000),
    )(fields, starts, labels)
    return out[0], out[1]


def solution(mesh):
    in_specs = (P(None, "space", None, None), P("arm", "space", None, None), P("arm"))
    out_specs = (P(None, "space", "arm", None), P(None, "space", "arm", None))
    return jax.shard_map(local, mesh=mesh, in_specs=in_specs, out_specs=out_specs, check_vma=False)
```

```python
import jax
import jax.numpy as jnp
from jax import lax
from jax.experimental import pallas as pl
from jax.experimental.pallas import tpu as pltpu
from jax.sharding import PartitionSpec as P

coupling_full = 0.15
contour_step = 0.05
chi_value = 2.0
mixing = 0.5
ARMS, NX, NY, NZ = 16, 256, 64, 128
MESH = pl.DeviceIdType.MESH


def stencil(ref, p, c):
    m = ref[p]
    s = ref[p - 1] + ref[p + 1]
    s = s + (pltpu.roll(m, 1, 0) + pltpu.roll(m, NY - 1, 0))
    s = s + (pltpu.roll(m, 1, 1) + pltpu.roll(m, NZ - 1, 1))
    return (1.0 / c - 6.0) * m + s


def contour(value, fac, base, count, u, w, u2, emit):
    for p in range(count):
        v = value(p)
        u[p] = fac(0, base + p) * v
        w[p] = fac(1, base + p) * v
    for p in range(1, count - 1):
        u2[p] = fac(2, base + p) * stencil(u, p, coupling_full / 2)
    for p in range(2, count - 2):
        h = fac(3, base + p) * stencil(u2, p, coupling_full / 2)
        f = fac(4, base + p) * stencil(w, p, coupling_full)
        emit(p, h - f)


def kernel(
    fields, starts, labels_hbm, out,
    labels, fld, st, fa, u, w, u2, step, f1s, rb, gs, g_in, gh, bo, b0, pr, chip_in, p2, x_in, jn, acc, d_in, zs, ys,
    local_sem, fld_s, fld_r, fc_s, fc_r, st_s, st_r, rb_s, rb_r, gi_s, gi_r, gh_s, gh_r, bo_s, bo_r, pc_s, pc_r, px_s, px_r,
    j_s, j_r, d_s, d_r, z_s, z_r, y_s, y_r, near_z, far_z, near_y, near_x,
):
    me_a, me_s = lax.axis_index("arm"), lax.axis_index("space")
    up, dn = lax.rem(me_s + 1, 64), lax.rem(me_s + 63, 64)
    core, high = lax.rem(me_a, 2), me_a // 2
    arm_c = high * 2 + 1 - core
    chip = (arm_c, me_s)
    across = ((1 - high) * 2 + core, me_s)
    cross = ((1 - high) * 2 + 1 - core, me_s)
    z = lax.rem(me_s, 8)
    row = me_s // 8
    y, x_lo = row // 2, lax.rem(row, 2)
    z_peer = [(me_a, me_s - z + lax.rem(z + k, 8)) for k in range(1, 8)]
    y_peer = [(me_a, me_s + (lax.rem(y + k, 4) - y) * 16) for k in range(1, 4)]
    x_s_id = me_s + 8 - 16 * x_lo
    x_peer = [(me_a, x_s_id), (arm_c, me_s), (arm_c, x_s_id)]
    wide_peer = y_peer + [
        (to[0], to[1] + (lax.rem(y + k, 4) - y) * 16) for to in x_peer for k in range(4)
    ]
    sides = [(me_a, up), (me_a, dn)]
    cross_sides = [(arm_c, up), (arm_c, dn)]

    def send(src, dst, ss, rs, to):
        return pltpu.make_async_remote_copy(src, dst, ss, rs, device_id=to, device_id_type=MESH)

    def signal(sem, to):
        pl.semaphore_signal(sem, inc=1, device_id=to, device_id_type=MESH)

    own_l = pltpu.make_async_copy(labels_hbm, labels, local_sem.at[5])
    own_l.start()
    own_f = pltpu.make_async_copy(fields, fld.at[:, pl.ds(4, 4)], local_sem.at[4])
    own_f.start()
    own = [pltpu.make_async_copy(starts.at[a], st.at[a, pl.ds(4, 4)], local_sem.at[a]) for a in range(4)]
    for c in own:
        c.start()

    barrier = pltpu.get_barrier_semaphore()
    near = [z_peer[0], z_peer[6]]
    peers = sides + cross_sides + [chip, across, cross] + near + [y_peer[0], y_peer[2], x_peer[0], x_peer[2]]
    for to in peers:
        signal(barrier, to)
    pl.semaphore_wait(barrier, len(peers))

    own_l.wait()
    own_f.wait()
    fld_c = [
        send(fld.at[core, pl.ds(4, 4)], fld.at[core, pl.ds(8 * i, 4)], fld_s.at[i], fld_r.at[i], sides[i])
        for i in range(2)
    ]
    for c in fld_c:
        c.start()

    def start_copy(a, i):
        return send(st.at[a, pl.ds(4, 4)], st.at[a, pl.ds(8 * i, 4)], st_s.at[a, i], st_r.at[a, i], sides[i])

    def end_copy(a, i):
        return send(
            rb.at[a, pl.ds(4 - 2 * i, 2)], rb.at[a, pl.ds(6 * i, 2)], rb_s.at[a, i], rb_r.at[a, i], sides[i]
        )

    for a in range(4):
        own[a].wait()
    for a in range(2):
        for i in range(2):
            start_copy(a, i).start()
    for to in near:
        signal(near_z, to)
    for k in (0, 2):
        signal(near_y, y_peer[k])
    pr[...] = jnp.ones_like(pr)
    gs[...] = jnp.zeros_like(gs)
    fc_c = [
        send(fld.at[core, pl.ds(8 * i, 4)], fld.at[core, pl.ds(8 * i, 4)], fc_s.at[i], fc_r.at[i], chip)
        for i in range(2)
    ]
    for i in range(2):
        fld_c[i].wait_recv()
        fc_c[i].start()
    for a in range(2, 4):
        for i in range(2):
            start_copy(a, i).start()

    pl.semaphore_wait(near_z, 2)
    for k in (1, 5):
        signal(far_z, z_peer[k])
    pl.semaphore_wait(near_y, 2)
    for to in x_peer:
        signal(near_x, to)
    for c in fc_c:
        c.wait_recv()

    def factor(p, _):
        for t in range(2):
            h = jnp.exp(fld[t, p] * (-contour_step / 4))
            f = h * h
            fa[t, 0, p] = h
            fa[t, 1, p] = f
            fa[t, 2, p] = (coupling_full / 2) * f
            fa[t, 3, p] = (4.0 / 3.0 * coupling_full / 2) * h
            fa[t, 4, p] = (1.0 / 3.0 * coupling_full) * f
        return 0

    lax.fori_loop(0, 12, factor, 0)

    def forward(a, _):
        lab = labels[a]
        is_a = lab == 0
        for i in range(2):
            start_copy(a, i).wait_recv()

        def keep_one(p, v):
            step[p] = v

        contour(lambda p: st[a, p], lambda i, p: fa[lab, i, p], 0, 12, u, w, u2, keep_one)

        def keep_two(p, v):
            own_p = p - 2
            f1s[a, own_p] = step[p + 2]
            r = 1.0 / v
            rb[a, p] = r
            pr[own_p] = pr[own_p] * v
            gs[0, p] = gs[0, p] + jnp.where(is_a, r, 0.0)
            gs[1, p] = gs[1, p] + jnp.where(is_a, 0.0, r)

        contour(
            lambda p: step[p + 2], lambda i, p: fa[lab, i, p], 2, 8, u, w, u2, keep_two
        )
        @pl.when(a < 3)
        def _():
            for i in range(2):
                end_copy(a, i).start()

        return 0

    lax.fori_loop(0, 4, forward, 0)

    mine = 2 * core
    pc = send(pr.at[pl.ds(2 - mine, 2)], chip_in, pc_s, pc_r, chip)
    pc.start()
    for i in range(2):
        end_copy(3, i).start()
    gi = send(gs.at[:, pl.ds(4 - mine, 2)], g_in, gi_s, gi_r, chip)
    pc.wait_recv()
    for k in range(2):
        p2[k] = pr[mine + k] * chip_in[k]
    px = send(p2, x_in, px_s, px_r, across)
    px.start()
    gi.start()
    pl.semaphore_wait(far_z, 2)
    px.wait_recv()
    total = jnp.zeros((8, NZ), jnp.float32)
    for k in range(2):
        j = p2[k] * x_in[k]
        jn[4 + mine + k] = j
        for q in range(8):
            total = total + j[8 * q : 8 * q + 8]

    near_side = core * up + (1 - core) * dn
    far_side = core * dn + (1 - core) * up
    half = pl.ds(4 + mine, 2)
    near_at = pl.ds(8 - 6 * core, 2)
    j_c = [
        send(jn.at[half], jn.at[near_at], j_s.at[0], j_r.at[0], (me_a, near_side)),
        send(jn.at[half], jn.at[near_at], j_s.at[1], j_r.at[1], (arm_c, near_side)),
        send(jn.at[half], jn.at[half], j_s.at[2], j_r.at[2], chip),
    ]
    for c in j_c:
        c.start()
    zs[0] = total
    z_c = [send(zs.at[0], zs.at[k + 1], z_s.at[k], z_r.at[k], z_peer[k]) for k in range(7)]
    for c in z_c:
        c.start()

    gi.wait_recv()
    for k in range(2):
        j = jn[4 + mine + k]
        for t in range(2):
            bo[t, k] = j * (gs[t, 2 + mine + k] + g_in[t, k])
        b0[4 + mine + k] = bo[core, k]
    far_at = pl.ds(10 * core, 2)
    bo_c = [
        send(bo.at[1 - core], b0.at[half], bo_s.at[2], bo_r.at[2], chip),
        send(bo.at[core], b0.at[far_at], bo_s.at[0], bo_r.at[0], (me_a, far_side)),
        send(bo.at[1 - core], b0.at[far_at], bo_s.at[1], bo_r.at[1], (arm_c, far_side)),
    ]
    for c in bo_c:
        c.start()

    for a in range(4):
        is_a = labels[a] == 0
        for i in range(2):
            end_copy(a, i).wait_recv()
        for p in (0, 1, 6, 7):
            r = rb[a, p]
            gs[0, p] = gs[0, p] + jnp.where(is_a, r, 0.0)
            gs[1, p] = gs[1, p] + jnp.where(is_a, 0.0, r)
    gh_c = [
        send(gs.at[1 - core, pl.ds(6 * i, 2)], gh.at[i], gh_s.at[i], gh_r.at[i], chip) for i in range(2)
    ]
    for c in gh_c:
        c.start()

    count_a = jnp.float32(0.0)
    for a in range(4):
        count_a = count_a + jnp.where(labels[a] == 0, 1.0, 0.0)

    def add(t, p, v):
        for b in range(4):
            acc[b, t, p] = acc[b, t, p] + v[16 * b : 16 * b + 16]

    j_c[2].wait_recv()
    for p in range(4):
        j = 0.25 * jn[4 + p]
        for b in range(4):
            acc[b, 0, p] = count_a * j[16 * b : 16 * b + 16]
            acc[b, 1, p] = (4.0 - count_a) * j[16 * b : 16 * b + 16]

    for c in j_c[:2]:
        c.wait_recv()

    for c in z_c:
        c.wait_recv()
    s = zs[0]
    for k in range(1, 8):
        s = s + zs[k]
    ys[0] = s
    pl.semaphore_wait(near_x, 3)
    y_c = [send(ys.at[0], ys.at[k + 1], y_s.at[k], y_r.at[k], wide_peer[k]) for k in range(15)]
    for c in y_c:
        c.start()
    def backward(a, _):
        lab = labels[a]
        is_a = lab == 0

        def middle(p, v):
            v = 0.5 * f1s[a, p - 2] * v
            add(0, p - 2, jnp.where(is_a, v, 0.0))
            add(1, p - 2, jnp.where(is_a, 0.0, v))

        contour(
            lambda p: jn[p + 2] * rb[a, p], lambda i, p: fa[lab, i, p], 2, 8, u, w, u2, middle
        )
        return 0

    lax.fori_loop(0, 4, backward, 0)
    owners = [across, cross, chip]

    def owner_copy(k, late):
        t = core if late else 1 - core
        return send(acc.at[owners[k][0], t], d_in.at[k, t], d_s.at[k, late], d_r.at[k, late], owners[k])

    for k in range(3):
        owner_copy(k, 0).start()
    for i in range(2):
        gh_c[i].wait_recv()
        for k in range(2):
            b0[2 + 6 * i + k] = jn[2 + 6 * i + k] * (gs[core, 6 * i + k] + gh[i, k])
    for c in bo_c:
        c.wait_recv()

    def keep_back(p, v):
        step[p] = v

    contour(
        lambda p: b0[p], lambda i, p: fa[core, i, p], 0, 12, u, w, u2, keep_back
    )

    def last(p, v):
        add(core, p - 2, 0.25 * v)

    contour(lambda p: step[p + 2], lambda i, p: fa[core, i, p], 2, 8, u, w, u2, last)

    for k in range(3):
        owner_copy(k, 1).start()
    for c in y_c:
        c.wait_recv()
    s = ys[0]
    for k in range(1, 16):
        s = s + ys[k]
    s = jnp.sum(jnp.sum(s, axis=0, keepdims=True), axis=1, keepdims=True)
    cells = float(NX * NY * NZ)
    scale = jnp.broadcast_to(1.0 / (ARMS * (s / cells)), (16, NZ))
    rows = pl.ds(pl.multiple_of(16 * me_a, 16), 16)
    for k in range(3):
        for late in range(2):
            owner_copy(k, late).wait_recv()
    for p in range(4):
        d = [
            scale * ((acc[me_a, t, p] + d_in[2, t, p]) + (d_in[0, t, p] + d_in[1, t, p])) for t in range(2)
        ]
        f = [fld[t, 4 + p, rows] for t in range(2)]
        pressure = 0.5 * (f[0] + f[1] - chi_value)
        for t in range(2):
            out[0, t, p] = d[t]
            out[1, t, p] = f[t] + mixing * (chi_value * d[1 - t] + pressure - f[t])
    for a in range(4):
        for i in range(2):
            start_copy(a, i).wait_send()
            end_copy(a, i).wait_send()
    for k in range(3):
        for late in range(2):
            owner_copy(k, late).wait_send()
    for c in fld_c + fc_c + [pc, gi, px] + gh_c + bo_c + j_c + z_c + y_c:
        c.wait_send()


def local(fields, starts, labels):
    vmem = lambda *shape: pltpu.VMEM(shape, jnp.float32)
    dma = lambda *shape: pltpu.SemaphoreType.DMA(shape)
    plane = (NY, NZ)
    out = pl.pallas_call(
        kernel,
        out_shape=jax.ShapeDtypeStruct((2, 2, 4, 16, NZ), jnp.float32),
        in_specs=[
            pl.BlockSpec(memory_space=pltpu.HBM),
            pl.BlockSpec(memory_space=pltpu.HBM),
            pl.BlockSpec(memory_space=pltpu.HBM),
        ],
        out_specs=pl.BlockSpec(memory_space=pltpu.VMEM),
        scratch_shapes=[
            pltpu.SMEM((4,), jnp.int32), vmem(2, 12, *plane), vmem(4, 12, *plane), vmem(2, 5, 12, *plane),
            vmem(12, *plane), vmem(12, *plane), vmem(12, *plane), vmem(12, *plane),
            vmem(4, 4, *plane), vmem(4, 8, *plane), vmem(2, 8, *plane), vmem(2, 2, *plane), vmem(2, 2, *plane), vmem(2, 2, *plane), vmem(12, *plane),
            vmem(4, *plane), vmem(2, *plane), vmem(2, *plane), vmem(2, *plane), vmem(12, *plane),
            vmem(4, 2, 4, 16, NZ), vmem(3, 2, 4, 16, NZ),
            vmem(8, 8, NZ), vmem(16, 8, NZ),
            dma(6), dma(2), dma(2), dma(2), dma(2), dma(4, 2), dma(4, 2), dma(4, 2), dma(4, 2),
            pltpu.SemaphoreType.DMA, pltpu.SemaphoreType.DMA, dma(2), dma(2), dma(3), dma(3),
            pltpu.SemaphoreType.DMA, pltpu.SemaphoreType.DMA, pltpu.SemaphoreType.DMA, pltpu.SemaphoreType.DMA,
            dma(3), dma(3), dma(3, 2), dma(3, 2), dma(7), dma(7), dma(15), dma(15),
            pltpu.SemaphoreType.REGULAR, pltpu.SemaphoreType.REGULAR, pltpu.SemaphoreType.REGULAR, pltpu.SemaphoreType.REGULAR,
        ],
        compiler_params=pltpu.CompilerParams(collective_id=0, has_side_effects=True, vmem_limit_bytes=56300000),
    )(fields, starts, labels)
    return out[0], out[1]


def solution(mesh):
    in_specs = (P(None, "space", None, None), P("arm", "space", None, None), P("arm"))
    out_specs = (P(None, "space", "arm", None), P(None, "space", "arm", None))
    return jax.shard_map(local, mesh=mesh, in_specs=in_specs, out_specs=out_specs, check_vma=False)
```
